256 devices in a mesh: wide: 64 (over x, z, y_lo), half: 4 (over y_hi, core).
Axes of the slice: x: 4, y: 4 (y_hi: 2, y_lo: 2; y = y_hi * 2 + y_lo), z: 8, core: 2. Of those that a mesh axis runs over, the one named last changes fastest.
Arguments:
- focus: bfloat16 [128, 3072, 512], P('half', 'wide'), may hold values from -6 to 6
- kernel: bfloat16 [64, 2, 3072, 3072], P('wide', None, 'half'), may hold values from -0.1875 to 0.1875
- onset: int32 [128], replicated, may hold values from 128 to 511
- tile_mask: int32 [12, 12], replicated, may hold values 0 or 1
Outputs:
- updated: bfloat16 [128, 3072, 512], P('half', 'wide')
The draws below stay inside these ranges and needn't reach their ends.
Inputs may be any that keep to these rules, and one draw needn't show every extreme that they name: `tile_mask`: 1 keeps a 256 x 256 block of the kernel, 0 removes it. Samples at and after the onset are muted.
All inputs are finite; a program needn't handle non-finite values.
Results may differ from the reference program's by a relative error of at most 0.012.
Values may be sent and summed in bfloat16 or wider, within the bound.
A program may use at most 128 MiB of HBM per device.

```python
import math
import jax
import jax.numpy as jnp
from jax import lax

NR = 3072
NT = 512
TILE = 256
NP = 128
NF = 64
N_HALF = 4


def touch_ends(result, own_key, least, high):
    index_at = [jax.random.randint(jax.random.fold_in(own_key, axis), (), 0, length) for axis, length in enumerate(result.shape)]
    longest = result.shape.index(max(result.shape))
    beside = index_at[:longest] + [(index_at[longest] + 1) % result.shape[longest]] + index_at[longest + 1:]
    return result.at[tuple(index_at)].set(least).at[tuple(beside)].set(high)


def level_of(stream_key, dims, split, smallest, high):
    def one(position, parts):
        draws = jax.random.uniform(jax.random.fold_in(jax.random.fold_in(stream_key, 6), position), (parts,), jnp.float32, smallest / len(split), high / len(split))
        return jnp.repeat(jnp.exp(draws), dims[position] // parts).reshape((-1,) + (1,) * (len(dims) - position - 1))

    level = one(*split[0])
    for cut in split[1:]:
        level = level * one(*cut)
    return level


def bell_draw(key, shape, scale, bound, pieces=(), kind=jnp.bfloat16):
    result = scale * jax.random.normal(key, shape, jnp.float32)
    if pieces:
        result = result * level_of(key, shape, pieces, -0.22, 0.18)
    return jnp.clip(result, -bound, bound).astype(kind)


def setup_inputs(seed: int = 0) -> dict:
    seeds = jax.random.split(jax.random.key(seed), 5)
    return {
        "focus": bell_draw(seeds[0], (NP, NR, NT), 1.0, 6.0, ((0, 4), (1, 64))),
        "kernel": bell_draw(seeds[1], (NF, 2, NR, NR), (3 * NF * NR // NT) ** -0.5, 0.1875, ((0, 64), (2, 4))),
        "onset": touch_ends(jax.random.randint(seeds[2], (NP,), NT // 4, NT), jax.random.fold_in(seeds[2], 1), NT // 4, NT - 1).astype(jnp.int32),
        "tile_mask": touch_ends((jax.random.randint(seeds[3], (NR // TILE, NR // TILE), 0, 4) < 3).astype(jnp.int32), jax.random.fold_in(seeds[3], 1), 0, 1),
    }


def make_tables(bins, length):
    times = jnp.arange(length, dtype=jnp.int32)
    number = jnp.arange(bins, dtype=jnp.int32) + 1
    phase = ((number[None, :] * times[:, None]) % length).astype(jnp.float32) * (2.0 * math.pi / length)
    table = jnp.stack([jnp.cos(phase), -jnp.sin(phase)], axis=2).reshape(length, 2 * bins)
    inverse = (table.T * (2.0 / length)).astype(jnp.bfloat16)
    return table.astype(jnp.bfloat16), inverse


def mask_kernel(kern, tile_mask):
    blocks = NR // TILE
    keeps = tile_mask.astype(jnp.bfloat16)
    shaped = kern.reshape(2, blocks, TILE, blocks, TILE) * keeps[None, :, None, :, None]
    return shaped.reshape(2, NR, NR)


def reference(focus, kernel, onset, tile_mask):
    forward_lookup_table, inverse_lookup_table = make_tables(NF, NT)
    spectra = jnp.dot(focus.reshape(NP * NR, NT), forward_lookup_table, preferred_element_type=jnp.float32)
    spectra = jnp.transpose(spectra.astype(jnp.bfloat16).reshape(NP, NR, NF, 2), (2, 3, 0, 1))

    def forward(pair):
        kern, values = pair
        masked = mask_kernel(kern, tile_mask)
        real_part = jnp.dot(values[0], masked[0].T, preferred_element_type=jnp.float32) - jnp.dot(values[1], masked[1].T, preferred_element_type=jnp.float32)
        imag_part = jnp.dot(values[1], masked[0].T, preferred_element_type=jnp.float32) + jnp.dot(values[0], masked[1].T, preferred_element_type=jnp.float32)
        return jnp.stack([real_part, imag_part]).astype(jnp.bfloat16)

    waves = lax.map(forward, (kernel, spectra))
    seismic_trace = jnp.dot(jnp.transpose(waves, (2, 3, 0, 1)).reshape(NP * NR, 2 * NF), inverse_lookup_table, preferred_element_type=jnp.float32).reshape(NP, NR, NT)
    live = jnp.arange(NT, dtype=jnp.int32)[None, None, :] < onset[:, None, None]
    muted_window = jnp.where(live, seismic_trace, 0.0).astype(jnp.bfloat16)
    returned = jnp.dot(muted_window.reshape(NP * NR, NT), forward_lookup_table, preferred_element_type=jnp.float32)
    returned = jnp.transpose(returned.astype(jnp.bfloat16).reshape(NP, NR, NF, 2), (2, 3, 0, 1))
    panel = NR // N_HALF

    def adjoint(pair):
        kern, values = pair
        masked = mask_kernel(kern, tile_mask)
        total_real = jnp.zeros((NP, NR), jnp.float32)
        total_imag = jnp.zeros((NP, NR), jnp.float32)
        for index in range(N_HALF):
            lower = index * panel
            kernel_real = masked[0, lower:lower + panel]
            kernel_imag = masked[1, lower:lower + panel]
            wave_real = values[0][:, lower:lower + panel]
            wave_imag = values[1][:, lower:lower + panel]
            real_part = jnp.dot(wave_real, kernel_real, preferred_element_type=jnp.float32) + jnp.dot(wave_imag, kernel_imag, preferred_element_type=jnp.float32)
            imag_part = jnp.dot(wave_imag, kernel_real, preferred_element_type=jnp.float32) - jnp.dot(wave_real, kernel_imag, preferred_element_type=jnp.float32)
            total_real = total_real + lax.optimization_barrier(real_part.astype(jnp.bfloat16)).astype(jnp.float32)
            total_imag = total_imag + lax.optimization_barrier(imag_part.astype(jnp.bfloat16)).astype(jnp.float32)
        return jnp.stack([total_real, total_imag]).astype(jnp.bfloat16)

    backward_pass = lax.map(adjoint, (kernel, returned))
    focusing_update = jnp.dot(jnp.transpose(backward_pass, (2, 3, 0, 1)).reshape(NP * NR, 2 * NF), inverse_lookup_table, preferred_element_type=jnp.float32).reshape(NP, NR, NT)
    return (focus.astype(jnp.float32) + jnp.where(live, focusing_update, 0.0)).astype(jnp.bfloat16)
```

```python
import functools

import jax
import jax.numpy as jnp
import numpy as np
from jax import lax
from jax.experimental import pallas as pl
from jax.experimental.pallas import tpu as pltpu
from jax.sharding import PartitionSpec as P

TILE = 256
NG = 4
GW = 16
CH = 24
F32 = jnp.float32
BF16 = jnp.bfloat16


def make_tables(bins, length):
    k = np.arange(1, bins + 1)
    t = np.arange(length)
    phase = (t[:, None] * k[None, :] % length).astype(np.float32) * np.float32(
        2.0 * np.pi / length
    )
    table = np.concatenate([np.cos(phase), -np.sin(phase)], axis=1)
    fwd = jnp.asarray(table, F32).astype(BF16)
    invt = jnp.asarray(table * (2.0 / length), F32).astype(BF16)
    return fwd, fwd.T, invt.T, invt


def wide_peer(me, d):
    x, loc = lax.div(me, GW), lax.rem(me, GW)
    i, n = lax.div(d, GW), lax.rem(d, GW)
    z, y = lax.div(loc, 2), lax.rem(loc, 2)
    tx = lax.rem(x + i, NG)
    tz = lax.rem(z + lax.div(n, 2), 8)
    ty = lax.rem(y + lax.rem(n, 2), 2)
    return tx * GW + tz * 2 + ty


def send(src, dst, ssem, rsem, wide, half):
    pltpu.make_async_remote_copy(
        src_ref=src,
        dst_ref=dst,
        send_sem=ssem,
        recv_sem=rsem,
        device_id={"wide": wide, "half": half},
        device_id_type=pl.DeviceIdType.MESH,
    ).start()


def await_bytes(ref, sem):
    pltpu.make_async_copy(ref, ref, sem).wait()


def focus_kernel(
    focus_hbm, kern_hbm, mask_ref, onset_ref, fwd_ref, fwdt_ref, invt_ref,
    out_ref,
    xv, mv, big, tr, v1, r1, fv, s2, r2, s3, h3, ht, pv, rs, qv, zs, zv, s4, r4,
    sem_x, sem_m, snd, rcv1, rel, rcv2, rcv3, rcvq, rcvz, rcv4, loc_sem,
):
    me = lax.axis_index("wide")
    hf = lax.axis_index("half")
    x = lax.div(me, GW)
    yh, q = lax.div(hf, 2), lax.rem(hf, 2)
    partner = yh * 2 + (1 - q)
    ypeer = (1 - yh) * 2 + q
    diag = (1 - yh) * 2 + (1 - q)
    copy_x = pltpu.make_async_copy(focus_hbm, xv, sem_x)
    copy_x.start()
    copy_m = pltpu.make_async_copy(kern_hbm, mv, sem_m)
    copy_m.start()
    barrier = pltpu.get_barrier_semaphore()

    @pl.loop(1, NG * GW)
    def _(d):
        pl.semaphore_signal(
            barrier,
            inc=1,
            device_id={"wide": wide_peer(me, d), "half": hf},
            device_id_type=pl.DeviceIdType.MESH,
        )

    for other in (partner, ypeer):
        pl.semaphore_signal(
            barrier,
            inc=1,
            device_id={"wide": me, "half": other},
            device_id_type=pl.DeviceIdType.MESH,
        )

    lane = lax.broadcasted_iota(jnp.int32, (1, 128), 1)
    low64 = lane < 64
    low32 = lax.rem(lane, 64) < 32

    copy_x.wait()
    for b in range(4):
        rows = pl.ds(b * 384, 384)
        big[rows, :] = jnp.dot(xv[rows, :], fwd_ref[...], preferred_element_type=F32)

    @pl.loop(0, 12)
    def _(jp):
        j = 2 * jp
        a = [
            [big[pl.ds(s * CH + j + jj, 32, stride=48), :] for jj in range(2)]
            for s in range(2)
        ]
        first = [jnp.where(low64, a[s][0], pltpu.roll(a[s][1], 64, 1)) for s in range(2)]
        second = [jnp.where(low64, pltpu.roll(a[s][0], 64, 1), a[s][1]) for s in range(2)]
        t = jnp.concatenate(first + second, axis=0).T
        tr[pl.ds(j, 64, stride=CH), :] = t[:64]
        tr[pl.ds(j + 1, 64, stride=CH), :] = t[64:]

    for b in range(4):
        v1[pl.ds(b * 16, 16)] = tr[pl.ds(b * 384, 384), :].astype(BF16).reshape(16, CH, 128)

    pl.semaphore_wait(barrier, NG * GW - 1 + 2)

    pltpu.make_async_copy(v1.at[me], r1.at[hf, me], rcv1.at[x]).start()

    @pl.loop(1, NG * GW)
    def _(d):
        peer = wide_peer(me, d)
        send(v1.at[peer], r1.at[hf, me], snd.at[0], rcv1.at[x], peer, hf)

    copy_m.wait()

    @pl.loop(0, 36)
    def _(n):
        a, b = lax.div(n, 12), lax.rem(n, 12)
        keep = mask_ref[hf * 3 + a, b].astype(F32)
        keep = jnp.full((TILE, TILE), keep, F32).astype(BF16)
        rows = pl.ds(pl.multiple_of(a * TILE, TILE), TILE)
        cols = pl.ds(pl.multiple_of(b * TILE, TILE), TILE)
        for c in range(2):
            mv[c, rows, cols] = mv[c, rows, cols] * keep

    def group(i):
        return lax.rem(x - i + NG, NG)

    def slab(g):
        return pl.ds(g * GW, GW)

    @pl.loop(0, NG)
    def _(i):
        g = group(i)
        own = r1.at[hf, slab(g)]
        await_bytes(own, rcv1.at[g])
        send(own, own, snd.at[1], rel.at[0, g], me, ypeer)
        send(own, own, snd.at[1], rel.at[1, g], me, partner)

    @pl.loop(0, NG)
    def _(i):
        g = group(i)
        theirs = r1.at[ypeer, slab(g)]
        await_bytes(theirs, rel.at[0, g])
        send(theirs, theirs, snd.at[1], rel.at[2, g], me, partner)

    @pl.loop(0, NG)
    def _(i):
        g = group(i)
        await_bytes(r1.at[partner, slab(g)], rel.at[1, g])
        await_bytes(r1.at[diag, slab(g)], rel.at[2, g])

        @pl.loop(0, GW)
        def _(n):
            w = g * GW + n
            rows = pl.ds(pl.multiple_of(w * 48, 48), 48)
            for t in range(2):
                b0 = r1[2 * t, w].astype(F32)
                b1 = r1[2 * t + 1, w].astype(F32)
                o0 = jnp.where(low32, b0, pltpu.roll(b1, 32, 1))
                o1 = jnp.where(low32, pltpu.roll(b0, 96, 1), b1)
                fv[rows, t * 128 : (t + 1) * 128] = jnp.concatenate([o0, o1], axis=0).astype(BF16)

    sign = jnp.where(low64, -1.0, 1.0).astype(F32)

    @pl.loop(0, NG)
    def _(i):
        b = lax.rem(x + i, NG)
        rows = pl.ds(pl.multiple_of(b * 192, 192), 192)
        lhs = jnp.concatenate([mv[0, rows, :], mv[1, rows, :]], axis=0)
        acc = jnp.dot(lhs, fv[...], preferred_element_type=F32)
        for t in range(2):
            re = acc[:192, t * 128 : (t + 1) * 128]
            im = acc[192:, t * 128 : (t + 1) * 128]
            wv = re + sign * pltpu.roll(im, 64, 1)
            s2[t, pl.ds(b * 8, 8)] = wv.astype(BF16).reshape(8, CH, 128)

        @pl.loop(0, GW)
        def _(n):
            peer = wide_peer(me, i * GW + n)
            src = s2.at[lax.rem(peer, 2), lax.div(peer, 2)]

            @pl.when(i + n > 0)
            def _():
                send(src, r2.at[me], snd.at[2], rcv2, peer, hf)

            @pl.when(i + n == 0)
            def _():
                pltpu.make_async_copy(src, r2.at[me], rcv2).start()

    await_bytes(r2, rcv2)

    for b in range(4):
        big[pl.ds(b * 384, 384), :] = r2[pl.ds(b * 16, 16)].astype(F32).reshape(384, 128)
    mine = onset_ref[pl.ds(lax.rem(me, 2), 1), :]
    mute = lax.broadcasted_iota(jnp.int32, (512, 128), 0) < mine
    mute = jnp.concatenate([mute, mute], axis=1)

    @pl.loop(0, 6)
    def _(rq):
        cols = []
        for u in range(2):
            r = rq * 4 + u * 2
            a0 = big[pl.ds(r, 64, stride=CH), :]
            a1 = big[pl.ds(r + 1, 64, stride=CH), :]
            top = jnp.where(low64, a0, pltpu.roll(a1, 64, 1))
            bot = jnp.where(low64, pltpu.roll(a0, 64, 1), a1)
            cols.append(jnp.concatenate([top, bot], axis=0))
        spec = jnp.concatenate(cols, axis=1).astype(BF16)
        trace = jnp.dot(invt_ref[...], spec, preferred_element_type=F32)
        muted = jnp.where(mute, trace, 0.0).astype(BF16)
        back = jnp.dot(fwdt_ref[...], muted, preferred_element_type=F32)
        for u in range(2):
            r = rq * 4 + u * 2
            top = back[:64, u * 128 : (u + 1) * 128]
            bot = back[64:, u * 128 : (u + 1) * 128]
            tr[pl.ds(r, 64, stride=CH), :] = jnp.where(low64, top, pltpu.roll(bot, 64, 1))
            tr[pl.ds(r + 1, 64, stride=CH), :] = jnp.where(low64, pltpu.roll(top, 64, 1), bot)

    for b in range(4):
        s3[pl.ds(b * 16, 16)] = tr[pl.ds(b * 384, 384), :].astype(BF16).reshape(16, CH, 128)
    slot = (lax.rem(me, 2), lax.div(me, 2))
    pltpu.make_async_copy(s3.at[me], h3.at[slot], rcv3).start()

    @pl.loop(1, NG * GW)
    def _(d):
        peer = wide_peer(me, d)
        send(s3.at[peer], h3.at[slot], snd.at[3], rcv3, peer, hf)

    await_bytes(h3, rcv3)

    for t in range(2):
        for b in range(2):
            piece = h3[t, pl.ds(b * 16, 16)].astype(F32).reshape(384, 128)
            for u in range(3):
                ht[t * 128 : (t + 1) * 128, b * 384 + u * 128 : b * 384 + (u + 1) * 128] = (
                    piece[u * 128 : (u + 1) * 128].T.astype(BF16)
                )

    @pl.loop(0, NG + 2)
    def _(i):
        @pl.when(i < NG)
        def _():
            g = lax.rem(x + i, NG)
            for b in range(3):
                cols = pl.ds(pl.multiple_of(g * 768 + b * TILE, TILE), TILE)
                pa = jnp.dot(ht[...], mv[0, :, cols], preferred_element_type=F32)
                pb = jnp.dot(ht[...], mv[1, :, cols], preferred_element_type=F32)
                pc = jnp.concatenate(
                    [
                        pa[0:64] + pb[64:128],
                        pa[64:128] - pb[0:64],
                        pa[128:192] + pb[192:256],
                        pa[192:256] - pb[128:192],
                    ],
                    axis=0,
                )
                pv[b * TILE : (b + 1) * TILE, :] = pc.T

            @pl.loop(0, GW)
            def _(n):
                w = g * GW + n
                for t in range(2):
                    base = pl.multiple_of(n * 48, 8)
                    i0 = pv[pl.ds(base, CH), t * 128 : (t + 1) * 128]
                    i1 = pv[pl.ds(pl.multiple_of(base + CH, 8), CH), t * 128 : (t + 1) * 128]
                    rs[2 * t, w] = jnp.where(low32, i0, pltpu.roll(i1, 32, 1)).astype(BF16)
                    rs[2 * t + 1, w] = jnp.where(low32, pltpu.roll(i0, 96, 1), i1).astype(BF16)

            for t in range(2):
                send(
                    rs.at[2 * t + (1 - q), slab(g)], qv.at[t, slab(g)],
                    snd.at[4], rcvq.at[t, g], me, partner,
                )

        @pl.when(jnp.logical_and(i >= 1, i <= NG))
        def _():
            g = lax.rem(x + i - 1, NG)
            t = 1 - yh
            await_bytes(qv.at[t, slab(g)], rcvq.at[t, g])
            total = rs[2 * t + q, slab(g)].astype(F32) + qv[t, slab(g)].astype(F32)
            zs[slab(g)] = total.astype(BF16)
            send(zs.at[slab(g)], zv.at[slab(g)], snd.at[5], rcvz.at[g], me, ypeer)

        @pl.when(i >= 2)
        def _():
            g = lax.rem(x + i - 2, NG)
            await_bytes(qv.at[yh, slab(g)], rcvq.at[yh, g])
            await_bytes(zv.at[slab(g)], rcvz.at[g])
            total = rs[hf, slab(g)].astype(F32) + qv[yh, slab(g)].astype(F32)
            s4[slab(g)] = (total + zv[slab(g)].astype(F32)).astype(BF16)

            @pl.loop(0, GW)
            def _(n):
                peer = wide_peer(me, (i - 2) * GW + n)

                @pl.when(i - 2 + n > 0)
                def _():
                    send(s4.at[peer], r4.at[me], snd.at[6], rcv4, peer, hf)

                @pl.when(i - 2 + n == 0)
                def _():
                    pltpu.make_async_copy(s4.at[peer], r4.at[me], rcv4).start()

    await_bytes(r4, rcv4)

    for b in range(4):
        big[pl.ds(b * 384, 384), :] = r4[pl.ds(b * 16, 16)].astype(F32).reshape(384, 128)

    @pl.loop(0, 12)
    def _(jp):
        j = 2 * jp
        a0 = big[pl.ds(j, 64, stride=CH), :]
        a1 = big[pl.ds(j + 1, 64, stride=CH), :]
        t = jnp.concatenate([a0, a1], axis=0).T
        l0 = jnp.where(low64, t[:64], pltpu.roll(t[64:], 64, 1))
        l1 = jnp.where(low64, pltpu.roll(t[:64], 64, 1), t[64:])
        for s in range(2):
            tr[pl.ds(s * CH + j, 32, stride=48), :] = l0[s * 32 : (s + 1) * 32]
            tr[pl.ds(s * CH + j + 1, 32, stride=48), :] = l1[s * 32 : (s + 1) * 32]

    for b in range(4):
        rows = pl.ds(b * 384, 384)
        out_ref[rows, :] = tr[rows, :].astype(BF16)

    n63 = pl.ds(0, NG * GW - 1)
    await_bytes(v1.at[n63], snd.at[0])
    await_bytes(r1.at[pl.ds(0, 3)], snd.at[1])
    await_bytes(r2.at[n63], snd.at[2])
    await_bytes(s3.at[n63], snd.at[3])
    await_bytes(rs.at[pl.ds(0, 2)], snd.at[4])
    await_bytes(zs, snd.at[5])
    await_bytes(s4.at[n63], snd.at[6])


def spectra_loop(focus, kern, tile_mask, onset2, fwd, fwdt, invt):
    dma = pltpu.SemaphoreType.DMA
    vmem = pl.BlockSpec(memory_space=pltpu.VMEM)
    hbm = pl.BlockSpec(memory_space=pl.ANY)
    smem = pl.BlockSpec(memory_space=pltpu.SMEM)
    chunk = (CH, 128)
    return pl.pallas_call(
        focus_kernel,
        out_shape=jax.ShapeDtypeStruct((1536, 128), BF16),
        in_specs=[hbm, hbm, smem, vmem, vmem, vmem, vmem],
        out_specs=vmem,
        scratch_shapes=[
            pltpu.VMEM((1536, 512), BF16),
            pltpu.VMEM((2, 768, 3072), BF16),
            pltpu.VMEM((1536, 128), F32),
            pltpu.VMEM((1536, 128), F32),
            pltpu.VMEM((64, *chunk), BF16),
            pltpu.VMEM((4, 64, *chunk), BF16),
            pltpu.VMEM((3072, 256), BF16),
            pltpu.VMEM((2, 32, *chunk), BF16),
            pltpu.VMEM((64, *chunk), BF16),
            pltpu.VMEM((64, *chunk), BF16),
            pltpu.VMEM((2, 32, *chunk), BF16),
            pltpu.VMEM((256, 768), BF16),
            pltpu.VMEM((768, 256), F32),
            pltpu.VMEM((4, 64, *chunk), BF16),
            pltpu.VMEM((2, 64, *chunk), BF16),
            pltpu.VMEM((64, *chunk), BF16),
            pltpu.VMEM((64, *chunk), BF16),
            pltpu.VMEM((64, *chunk), BF16),
            pltpu.VMEM((64, *chunk), BF16),
            dma, dma, dma((7,)), dma((NG,)), dma((3, NG)), dma, dma,
            dma((2, NG)), dma((NG,)), dma, dma,
        ],
        compiler_params=pltpu.CompilerParams(
            collective_id=0, has_side_effects=True, vmem_limit_bytes=60 * 1024 * 1024
        ),
        name="focus_update",
    )(focus, kern, tile_mask, onset2, fwd, fwdt, invt)


def finish_kernel(points, onset_ref, spec_ref, focus_ref, inv_ref, out_ref):
    i = pl.program_id(0)
    upd = jnp.dot(spec_ref[...], inv_ref[...], preferred_element_type=F32)
    time = lax.broadcasted_iota(jnp.int32, (48, 512), 1)
    for n in range(points):
        kept = jnp.where(time < onset_ref[i * points + n], upd[n * 48 : (n + 1) * 48], 0.0)
        out_ref[n] = (focus_ref[n].astype(F32) + kept).astype(BF16)


def finish(onset, spec, focus, inv):
    points = 8
    return pl.pallas_call(
        functools.partial(finish_kernel, points),
        out_shape=jax.ShapeDtypeStruct(focus.shape, BF16),
        grid=(32 // points,),
        in_specs=[
            pl.BlockSpec(memory_space=pltpu.SMEM),
            pl.BlockSpec((points * 48, 128), lambda i: (i, 0)),
            pl.BlockSpec((points, 48, 512), lambda i: (i, 0, 0)),
            pl.BlockSpec((128, 512), lambda i: (0, 0)),
        ],
        out_specs=pl.BlockSpec((points, 48, 512), lambda i: (i, 0, 0)),
        name="finish",
    )(onset, spec, focus, inv)


def shards(focus, kernel, onset, tile_mask):
    own_points, local_receivers, length = focus.shape
    fwd, fwdt, inv, invt = make_tables(64, length)
    halves = onset.reshape(2, 64)
    spec = spectra_loop(
        focus.reshape(own_points * local_receivers, length),
        kernel[0],
        tile_mask,
        jnp.concatenate([halves, halves], axis=1),
        fwd, fwdt, invt,
    )
    mine = lax.dynamic_slice_in_dim(onset, lax.axis_index("half") * own_points, own_points, 0)
    return finish(mine, spec, focus, inv)


def solution(mesh):
    in_specs = (P("half", "wide", None), P("wide", None, "half", None), P(), P())
    out_specs = P("half", "wide", None)
    return jax.shard_map(shards, mesh=mesh, in_specs=in_specs, out_specs=out_specs, check_vma=False)
```

```python
import functools

import jax
import jax.numpy as jnp
import numpy as np
from jax import lax
from jax.experimental import pallas as pl
from jax.experimental.pallas import tpu as pltpu
from jax.sharding import PartitionSpec as P

TILE = 256
NG = 4
GW = 16
CH = 24
F32 = jnp.float32
BF16 = jnp.bfloat16


def make_tables(bins, length):
    k = np.arange(1, bins + 1)
    t = np.arange(length)
    phase = (t[:, None] * k[None, :] % length).astype(np.float32) * np.float32(
        2.0 * np.pi / length
    )
    table = np.concatenate([np.cos(phase), -np.sin(phase)], axis=1)
    fwd = jnp.asarray(table, F32).astype(BF16)
    invt = jnp.asarray(table * (2.0 / length), F32).astype(BF16)
    return fwd, fwd.T, invt.T, invt


def wide_peer(me, d):
    x, loc = lax.div(me, GW), lax.rem(me, GW)
    i, n = lax.div(d, GW), lax.rem(d, GW)
    z, y = lax.div(loc, 2), lax.rem(loc, 2)
    tx = lax.rem(x + i, NG)
    tz = lax.rem(z + lax.div(n, 2), 8)
    ty = lax.rem(y + lax.rem(n, 2), 2)
    return tx * GW + tz * 2 + ty


def send(src, dst, ssem, rsem, wide, half):
    pltpu.make_async_remote_copy(
        src_ref=src,
        dst_ref=dst,
        send_sem=ssem,
        recv_sem=rsem,
        device_id={"wide": wide, "half": half},
        device_id_type=pl.DeviceIdType.MESH,
    ).start()


def await_bytes(ref, sem):
    pltpu.make_async_copy(ref, ref, sem).wait()


def focus_kernel(
    focus_hbm, kern_hbm, mask_ref, onset_ref, fwd_ref, fwdt_ref, invt_ref,
    out_ref,
    xv, mv, big, tr, v1, b1, r1, fv, acc, s2, r2, s3, h3, ht, pv, rs, qv, zs, zr, s4, r4,
    sem_x, sem_m, snd, rcva, rcvb, rel, chip, rcv2, rcv3, rcvq, rcvz, rcv4,
):
    me = lax.axis_index("wide")
    hf = lax.axis_index("half")
    x = lax.div(me, GW)
    yh, q = lax.div(hf, 2), lax.rem(hf, 2)
    partner = yh * 2 + (1 - q)
    ypeer = (1 - yh) * 2 + q
    z, yl = lax.div(lax.rem(me, GW), 2), lax.rem(me, 2)
    beside = x * GW + 2 * z + (1 - yl)
    copy_x = pltpu.make_async_copy(focus_hbm, xv, sem_x)
    copy_x.start()
    copy_m = pltpu.make_async_copy(kern_hbm, mv, sem_m)
    copy_m.start()
    barrier = pltpu.get_barrier_semaphore()

    @pl.loop(1, NG * GW)
    def _(d):
        pl.semaphore_signal(
            barrier,
            inc=1,
            device_id={"wide": wide_peer(me, d), "half": hf},
            device_id_type=pl.DeviceIdType.MESH,
        )

    for w, other in ((me, partner), (me, ypeer), (beside, ypeer)):
        pl.semaphore_signal(
            barrier,
            inc=1,
            device_id={"wide": w, "half": other},
            device_id_type=pl.DeviceIdType.MESH,
        )

    lane = lax.broadcasted_iota(jnp.int32, (1, 128), 1)
    low64 = lane < 64
    low32 = lax.rem(lane, 64) < 32

    copy_x.wait()
    for b in range(4):
        rows = pl.ds(b * 384, 384)
        big[rows, :] = jnp.dot(xv[rows, :], fwd_ref[...], preferred_element_type=F32)

    @pl.loop(0, 12)
    def _(jp):
        j = 2 * jp
        a = [
            [big[pl.ds(s * CH + j + jj, 32, stride=48), :] for jj in range(2)]
            for s in range(2)
        ]
        first = [jnp.where(low64, a[s][0], pltpu.roll(a[s][1], 64, 1)) for s in range(2)]
        second = [jnp.where(low64, pltpu.roll(a[s][0], 64, 1), a[s][1]) for s in range(2)]
        t = jnp.concatenate(first + second, axis=0).T
        tr[pl.ds(j, 64, stride=CH), :] = t[:64]
        tr[pl.ds(j + 1, 64, stride=CH), :] = t[64:]

    for b in range(4):
        v1[pl.ds(b * 16, 16)] = tr[pl.ds(b * 384, 384), :].astype(BF16).reshape(16, CH, 128)

    pl.semaphore_wait(barrier, NG * GW - 1 + 3)

    here = x * 8 + z
    own_k = here * 2
    pltpu.make_async_copy(v1.at[me], r1.at[hf, x, yl, z], rcva.at[x]).start()
    pltpu.make_async_copy(v1.at[own_k + 1 - yl], b1.at[here], rcvb.at[x]).start()

    @pl.loop(1, 32)
    def _(d):
        tx = lax.rem(x + lax.div(d, 8), NG)
        tz = lax.rem(z + lax.rem(d, 8), 8)
        k = tx * GW + tz * 2
        peer = k + yl
        send(v1.at[peer], r1.at[hf, x, yl, z], snd.at[0], rcva.at[x], peer, hf)
        send(v1.at[k + 1 - yl], b1.at[here], snd.at[0], rcvb.at[x], peer, hf)

    copy_m.wait()

    @pl.loop(0, 36)
    def _(n):
        a, b = lax.div(n, 12), lax.rem(n, 12)
        keep = mask_ref[hf * 3 + a, b].astype(F32)
        keep = jnp.full((TILE, TILE), keep, F32).astype(BF16)
        rows = pl.ds(pl.multiple_of(a * TILE, TILE), TILE)
        cols = pl.ds(pl.multiple_of(b * TILE, TILE), TILE)
        for c in range(2):
            mv[c, rows, cols] = mv[c, rows, cols] * keep

    acc[...] = jnp.zeros_like(acc)
    sign = jnp.where(low64, -1.0, 1.0).astype(F32)

    def slab(g):
        return pl.ds(g * 8, 8)

    def product(g, b):
        rows = pl.ds(pl.multiple_of(b * 192, 192), 192)
        cols = pl.ds(pl.multiple_of(g * 768, 768), 768)
        lhs = jnp.concatenate([mv[0, rows, cols], mv[1, rows, cols]], axis=0)
        return jnp.dot(lhs, fv[...], preferred_element_type=F32)

    @pl.loop(0, NG + 2)
    def _(i):
        @pl.when(i < NG)
        def _():
            g = lax.rem(x - i + NG, NG)
            own = r1.at[hf, g, yl]
            await_bytes(own, rcva.at[g])
            send(own, own, snd.at[1], rel.at[0, g], me, ypeer)
            send(own, own, snd.at[2], chip.at[0, g], me, partner)
            await_bytes(b1.at[slab(g)], rcvb.at[g])
            send(b1.at[slab(g)], own, snd.at[1], rel.at[1, g], beside, hf)
            send(b1.at[slab(g)], own, snd.at[1], rel.at[2, g], beside, ypeer)

        @pl.when(jnp.logical_and(i >= 1, i <= NG))
        def _():
            g = lax.rem(x - i + 1 + NG, NG)
            for n, (h, y) in enumerate(((ypeer, yl), (hf, 1 - yl), (ypeer, 1 - yl))):
                got = r1.at[h, g, y]
                await_bytes(got, rel.at[n, g])
                send(got, got, snd.at[2], chip.at[n + 1, g], me, partner)

        @pl.when(i >= 2)
        def _():
            g = lax.rem(x - i + 2 + NG, NG)
            diag = (1 - yh) * 2 + (1 - q)
            for n, (h, y) in enumerate(
                ((partner, yl), (diag, yl), (partner, 1 - yl), (diag, 1 - yl))
            ):
                await_bytes(r1.at[h, g, y], chip.at[n, g])

            @pl.loop(0, GW)
            def _(n):
                at = (lax.rem(n, 2), lax.div(n, 2))
                rows = pl.ds(pl.multiple_of(n * 48, 48), 48)
                for t in range(2):
                    b0 = r1[2 * t, g, at[0], at[1]].astype(F32)
                    b1_ = r1[2 * t + 1, g, at[0], at[1]].astype(F32)
                    o0 = jnp.where(low32, b0, pltpu.roll(b1_, 32, 1))
                    o1 = jnp.where(low32, pltpu.roll(b0, 96, 1), b1_)
                    fv[rows, t * 128 : (t + 1) * 128] = jnp.concatenate([o0, o1], axis=0).astype(BF16)

            @pl.when(i < NG + 1)
            def _():
                @pl.loop(0, NG)
                def _(b):
                    acc[b] += product(g, b)

    @pl.loop(0, NG)
    def _(i):
        b = lax.rem(x + i, NG)
        full = acc[b] + product(lax.rem(x + 1, NG), b)
        for t in range(2):
            re = full[:192, t * 128 : (t + 1) * 128]
            im = full[192:, t * 128 : (t + 1) * 128]
            wv = re + sign * pltpu.roll(im, 64, 1)
            s2[t, pl.ds(b * 8, 8)] = wv.astype(BF16).reshape(8, CH, 128)

        @pl.loop(0, GW)
        def _(n):
            peer = wide_peer(me, i * GW + n)
            src = s2.at[lax.rem(peer, 2), lax.div(peer, 2)]

            @pl.when(i + n > 0)
            def _():
                send(src, r2.at[me], snd.at[3], rcv2, peer, hf)

            @pl.when(i + n == 0)
            def _():
                pltpu.make_async_copy(src, r2.at[me], rcv2).start()

    await_bytes(r2, rcv2)

    for b in range(4):
        big[pl.ds(b * 384, 384), :] = r2[pl.ds(b * 16, 16)].astype(F32).reshape(384, 128)
    points = jnp.broadcast_to(onset_ref[...], (8, 128))
    other = pltpu.roll(points, 64, 1)
    mine = jnp.where(
        yl == 0, jnp.where(low64, points, other), jnp.where(low64, other, points)
    )[0:1]
    mute = lax.broadcasted_iota(jnp.int32, (512, 128), 0) < mine
    mute = jnp.concatenate([mute, mute], axis=1)

    @pl.loop(0, 6)
    def _(rq):
        cols = []
        for u in range(2):
            r = rq * 4 + u * 2
            a0 = big[pl.ds(r, 64, stride=CH), :]
            a1 = big[pl.ds(r + 1, 64, stride=CH), :]
            top = jnp.where(low64, a0, pltpu.roll(a1, 64, 1))
            bot = jnp.where(low64, pltpu.roll(a0, 64, 1), a1)
            cols.append(jnp.concatenate([top, bot], axis=0))
        spec = jnp.concatenate(cols, axis=1).astype(BF16)
        trace = jnp.dot(invt_ref[...], spec, preferred_element_type=F32)
        muted = jnp.where(mute, trace, 0.0).astype(BF16)
        back = jnp.dot(fwdt_ref[...], muted, preferred_element_type=F32)
        for u in range(2):
            r = rq * 4 + u * 2
            top = back[:64, u * 128 : (u + 1) * 128]
            bot = back[64:, u * 128 : (u + 1) * 128]
            tr[pl.ds(r, 64, stride=CH), :] = jnp.where(low64, top, pltpu.roll(bot, 64, 1))
            tr[pl.ds(r + 1, 64, stride=CH), :] = jnp.where(low64, pltpu.roll(top, 64, 1), bot)

    for b in range(4):
        s3[pl.ds(b * 16, 16)] = tr[pl.ds(b * 384, 384), :].astype(BF16).reshape(16, CH, 128)
    slot = (lax.rem(me, 2), lax.div(me, 2))
    pltpu.make_async_copy(s3.at[me], h3.at[slot], rcv3).start()

    @pl.loop(1, NG * GW)
    def _(d):
        peer = wide_peer(me, d)
        send(s3.at[peer], h3.at[slot], snd.at[4], rcv3, peer, hf)

    await_bytes(h3, rcv3)

    for t in range(2):
        for b in range(2):
            piece = h3[t, pl.ds(b * 16, 16)].astype(F32).reshape(384, 128)
            for u in range(3):
                ht[t * 128 : (t + 1) * 128, b * 384 + u * 128 : b * 384 + (u + 1) * 128] = (
                    piece[u * 128 : (u + 1) * 128].T.astype(BF16)
                )

    @pl.loop(0, NG + 2)
    def _(i):
        @pl.when(i < NG)
        def _():
            g = lax.rem(x + i, NG)
            for b in range(3):
                cols = pl.ds(pl.multiple_of(g * 768 + b * TILE, TILE), TILE)
                pa = jnp.dot(ht[...], mv[0, :, cols], preferred_element_type=F32)
                pb = jnp.dot(ht[...], mv[1, :, cols], preferred_element_type=F32)
                pc = jnp.concatenate(
                    [
                        pa[0:64] + pb[64:128],
                        pa[64:128] - pb[0:64],
                        pa[128:192] + pb[192:256],
                        pa[192:256] - pb[128:192],
                    ],
                    axis=0,
                )
                pv[b * TILE : (b + 1) * TILE, :] = pc.T

            @pl.loop(0, GW)
            def _(n):
                y, zz = lax.rem(n, 2), lax.div(n, 2)
                for t in range(2):
                    base = pl.multiple_of(n * 48, 8)
                    i0 = pv[pl.ds(base, CH), t * 128 : (t + 1) * 128]
                    i1 = pv[pl.ds(pl.multiple_of(base + CH, 8), CH), t * 128 : (t + 1) * 128]
                    rs[2 * t, g, y, zz] = jnp.where(low32, i0, pltpu.roll(i1, 32, 1)).astype(BF16)
                    rs[2 * t + 1, g, y, zz] = jnp.where(low32, pltpu.roll(i0, 96, 1), i1).astype(BF16)

            for t in range(2):
                send(rs.at[2 * t + (1 - q), g], qv.at[t, g], snd.at[5], rcvq.at[t, g], me, partner)

        @pl.when(jnp.logical_and(i >= 1, i <= NG))
        def _():
            g = lax.rem(x + i - 1, NG)
            for t in range(2):
                await_bytes(qv.at[t, g], rcvq.at[t, g])
                total = rs[2 * t + q, g].astype(F32) + qv[t, g].astype(F32)
                zs[t, g] = total.astype(BF16)
            send(zs.at[1 - yh, g, 1 - yl], zr.at[2, g], snd.at[6], rcvz.at[2, g], beside, ypeer)
            send(zs.at[yh, g, 1 - yl], zr.at[1, g], snd.at[6], rcvz.at[1, g], beside, hf)
            send(zs.at[1 - yh, g, yl], zr.at[0, g], snd.at[6], rcvz.at[0, g], me, ypeer)

        @pl.when(i >= 2)
        def _():
            g = lax.rem(x + i - 2, NG)
            for n in range(3):
                await_bytes(zr.at[n, g], rcvz.at[n, g])
            s4[yl, g] = (zs[yh, g, yl].astype(F32) + zr[0, g].astype(F32)).astype(BF16)
            s4[1 - yl, g] = (zr[1, g].astype(F32) + zr[2, g].astype(F32)).astype(BF16)

            @pl.loop(0, 8)
            def _(n):
                tz = lax.rem(z + n, 8)
                peer = g * GW + tz * 2 + yl
                k = x * GW + z * 2

                @pl.when(i - 2 + n > 0)
                def _():
                    send(s4.at[0, g, tz], r4.at[k], snd.at[7], rcv4, peer, hf)
                    send(s4.at[1, g, tz], r4.at[k + 1], snd.at[7], rcv4, peer, hf)

                @pl.when(i - 2 + n == 0)
                def _():
                    pltpu.make_async_copy(s4.at[0, g, tz], r4.at[k], rcv4).start()
                    pltpu.make_async_copy(s4.at[1, g, tz], r4.at[k + 1], rcv4).start()

    await_bytes(r4, rcv4)

    for b in range(4):
        big[pl.ds(b * 384, 384), :] = r4[pl.ds(b * 16, 16)].astype(F32).reshape(384, 128)

    @pl.loop(0, 12)
    def _(jp):
        j = 2 * jp
        a0 = big[pl.ds(j, 64, stride=CH), :]
        a1 = big[pl.ds(j + 1, 64, stride=CH), :]
        t = jnp.concatenate([a0, a1], axis=0).T
        l0 = jnp.where(low64, t[:64], pltpu.roll(t[64:], 64, 1))
        l1 = jnp.where(low64, pltpu.roll(t[:64], 64, 1), t[64:])
        for s in range(2):
            tr[pl.ds(s * CH + j, 32, stride=48), :] = l0[s * 32 : (s + 1) * 32]
            tr[pl.ds(s * CH + j + 1, 32, stride=48), :] = l1[s * 32 : (s + 1) * 32]

    for b in range(4):
        rows = pl.ds(b * 384, 384)
        out_ref[rows, :] = tr[rows, :].astype(BF16)

    n63 = pl.ds(0, NG * GW - 1)
    await_bytes(v1.at[pl.ds(0, 62)], snd.at[0])
    await_bytes(rs.at[pl.ds(0, 3), :, 0], snd.at[1])
    await_bytes(rs.at[pl.ds(0, 2)], snd.at[2])
    await_bytes(r2.at[n63], snd.at[3])
    await_bytes(s3.at[n63], snd.at[4])
    await_bytes(rs.at[pl.ds(0, 2)], snd.at[5])
    await_bytes(zr, snd.at[6])
    await_bytes(r4.at[pl.ds(0, 62)], snd.at[7])


def spectra_loop(focus, kern, tile_mask, onset2, fwd, fwdt, invt):
    dma = pltpu.SemaphoreType.DMA
    vmem = pl.BlockSpec(memory_space=pltpu.VMEM)
    hbm = pl.BlockSpec(memory_space=pl.ANY)
    smem = pl.BlockSpec(memory_space=pltpu.SMEM)
    chunk = (CH, 128)
    return pl.pallas_call(
        focus_kernel,
        out_shape=jax.ShapeDtypeStruct((1536, 128), BF16),
        in_specs=[hbm, hbm, smem, vmem, vmem, vmem, vmem],
        out_specs=vmem,
        scratch_shapes=[
            pltpu.VMEM((1536, 512), BF16),
            pltpu.VMEM((2, 768, 3072), BF16),
            pltpu.VMEM((1536, 128), F32),
            pltpu.VMEM((1536, 128), F32),
            pltpu.VMEM((64, *chunk), BF16),
            pltpu.VMEM((32, *chunk), BF16),
            pltpu.VMEM((4, NG, 2, 8, *chunk), BF16),
            pltpu.VMEM((768, 256), BF16),
            pltpu.VMEM((NG, 384, 256), F32),
            pltpu.VMEM((2, 32, *chunk), BF16),
            pltpu.VMEM((64, *chunk), BF16),
            pltpu.VMEM((64, *chunk), BF16),
            pltpu.VMEM((2, 32, *chunk), BF16),
            pltpu.VMEM((256, 768), BF16),
            pltpu.VMEM((768, 256), F32),
            pltpu.VMEM((4, NG, 2, 8, *chunk), BF16),
            pltpu.VMEM((2, NG, 2, 8, *chunk), BF16),
            pltpu.VMEM((2, NG, 2, 8, *chunk), BF16),
            pltpu.VMEM((3, NG, 8, *chunk), BF16),
            pltpu.VMEM((2, NG, 8, *chunk), BF16),
            pltpu.VMEM((64, *chunk), BF16),
            dma, dma, dma((8,)), dma((NG,)), dma((NG,)), dma((3, NG)), dma((4, NG)),
            dma, dma, dma((2, NG)), dma((3, NG)), dma,
        ],
        compiler_params=pltpu.CompilerParams(
            collective_id=0, has_side_effects=True, vmem_limit_bytes=60 * 1024 * 1024
        ),
        name="focus_update",
    )(focus, kern, tile_mask, onset2, fwd, fwdt, invt)


def finish_kernel(points, onset_ref, spec_ref, focus_ref, inv_ref, out_ref):
    i = pl.program_id(0)
    first = lax.axis_index("half") * 32 + i * points
    upd = jnp.dot(spec_ref[...], inv_ref[...], preferred_element_type=F32)
    time = lax.broadcasted_iota(jnp.int32, (48, 512), 1)
    for n in range(points):
        kept = jnp.where(time < onset_ref[first + n], upd[n * 48 : (n + 1) * 48], 0.0)
        out_ref[n] = (focus_ref[n].astype(F32) + kept).astype(BF16)


def finish(onset, spec, focus, inv):
    points = 8
    return pl.pallas_call(
        functools.partial(finish_kernel, points),
        out_shape=jax.ShapeDtypeStruct(focus.shape, BF16),
        grid=(32 // points,),
        in_specs=[
            pl.BlockSpec(memory_space=pltpu.SMEM),
            pl.BlockSpec((points * 48, 128), lambda i: (i, 0)),
            pl.BlockSpec((points, 48, 512), lambda i: (i, 0, 0)),
            pl.BlockSpec((128, 512), lambda i: (0, 0)),
        ],
        out_specs=pl.BlockSpec((points, 48, 512), lambda i: (i, 0, 0)),
        name="finish",
    )(onset, spec, focus, inv)


def shards(focus, kernel, onset, tile_mask):
    own_points, local_receivers, length = focus.shape
    fwd, fwdt, inv, invt = make_tables(64, length)
    spec = spectra_loop(
        focus.reshape(own_points * local_receivers, length),
        kernel[0],
        tile_mask,
        onset.reshape(1, 128),
        fwd, fwdt, invt,
    )
    return finish(onset, spec, focus, inv)


def solution(mesh):
    in_specs = (P("half", "wide", None), P("wide", None, "half", None), P(), P())
    out_specs = P("half", "wide", None)
    return jax.shard_map(shards, mesh=mesh, in_specs=in_specs, out_specs=out_specs, check_vma=False)
```

```python
import functools

import jax
import jax.numpy as jnp
import numpy as np
from jax import lax
from jax.experimental import pallas as pl
from jax.experimental.pallas import tpu as pltpu
from jax.sharding import PartitionSpec as P

TILE = 256
NG = 4
GW = 16
CH = 24
F32 = jnp.float32
BF16 = jnp.bfloat16


def make_tables(bins, length):
    k = np.arange(1, bins + 1)
    t = np.arange(length)
    phase = (t[:, None] * k[None, :] % length).astype(np.float32) * np.float32(
        2.0 * np.pi / length
    )
    table = np.concatenate([np.cos(phase), -np.sin(phase)], axis=1)
    fwd = jnp.asarray(table, F32).astype(BF16)
    invt = jnp.asarray(table * (2.0 / length), F32).astype(BF16)
    return fwd, fwd.T, invt.T, invt


def z_step(n):
    m = lax.div(n, 2)
    return jnp.where(n < 2, 4 * n, jnp.where(lax.rem(n, 2) == 0, m, 8 - m))


def wide_peer(me, d):
    x, loc = lax.div(me, GW), lax.rem(me, GW)
    i, n = lax.div(d, GW), lax.rem(d, GW)
    z, y = lax.div(loc, 2), lax.rem(loc, 2)
    tx = lax.rem(x + i, NG)
    tz = lax.rem(z + z_step(lax.div(n, 2)), 8)
    ty = lax.rem(y + lax.rem(n, 2), 2)
    return tx * GW + tz * 2 + ty


def send(src, dst, ssem, rsem, wide, half):
    pltpu.make_async_remote_copy(
        src_ref=src,
        dst_ref=dst,
        send_sem=ssem,
        recv_sem=rsem,
        device_id={"wide": wide, "half": half},
        device_id_type=pl.DeviceIdType.MESH,
    ).start()


def await_bytes(ref, sem):
    pltpu.make_async_copy(ref, ref, sem).wait()


def focus_kernel(
    focus_hbm, kern_hbm, mask_ref, onset_hbm, onset_smem, fwd_hbm, fwdt_hbm, inv_hbm, invt_hbm,
    out_ref,
    onset_ref, fwd_ref, fwdt_ref, inv_ref, invt_ref, xv, mv, big, tr, v1, b1, r1, fv, acc, s2, r2, s3, h3, ht, pv, rs, qv, zs, zr, s4, r4,
    sem_t, sem_x, sem_m, snd, first, rcva, rcvb, rel, chip, rcv2, rcv3, rcvq, rcvz, rcv4,
):
    me = lax.axis_index("wide")
    hf = lax.axis_index("half")
    x = lax.div(me, GW)
    yh, q = lax.div(hf, 2), lax.rem(hf, 2)
    partner = yh * 2 + (1 - q)
    ypeer = (1 - yh) * 2 + q
    z, yl = lax.div(lax.rem(me, GW), 2), lax.rem(me, 2)
    beside = x * GW + 2 * z + (1 - yl)
    barrier = pltpu.get_barrier_semaphore()

    @pl.loop(1, NG * GW)
    def _(d):
        pl.semaphore_signal(
            barrier,
            inc=1,
            device_id={"wide": wide_peer(me, d), "half": hf},
            device_id_type=pl.DeviceIdType.MESH,
        )

    for w, other in ((me, partner), (me, ypeer), (beside, ypeer)):
        pl.semaphore_signal(
            barrier,
            inc=1,
            device_id={"wide": w, "half": other},
            device_id_type=pl.DeviceIdType.MESH,
        )

    tables = [
        pltpu.make_async_copy(src, dst, sem_t.at[n])
        for n, (src, dst) in enumerate(
            (
                (fwd_hbm, fwd_ref), (fwdt_hbm, fwdt_ref), (inv_hbm, inv_ref),
                (invt_hbm, invt_ref), (onset_hbm, onset_ref),
            )
        )
    ]
    tables[0].start()
    copy_x = pltpu.make_async_copy(focus_hbm, xv, sem_x)
    copy_x.start()
    copy_m = pltpu.make_async_copy(kern_hbm, mv, sem_m)
    copy_m.start()
    for table in tables[1:]:
        table.start()

    lane = lax.broadcasted_iota(jnp.int32, (1, 128), 1)
    low64 = lane < 64
    low32 = lax.rem(lane, 64) < 32

    tables[0].wait()
    copy_x.wait()
    for b in range(4):
        rows = pl.ds(b * 384, 384)
        big[rows, :] = jnp.dot(xv[rows, :], fwd_ref[...], preferred_element_type=F32)

    @pl.loop(0, 12, unroll=4)
    def _(jp):
        j = 2 * jp
        a = [
            [big[pl.ds(s * CH + j + jj, 32, stride=48), :] for jj in range(2)]
            for s in range(2)
        ]
        even = [jnp.where(low64, a[s][0], pltpu.roll(a[s][1], 64, 1)) for s in range(2)]
        odd = [jnp.where(low64, pltpu.roll(a[s][0], 64, 1), a[s][1]) for s in range(2)]
        t = jnp.concatenate(even + odd, axis=0).T
        tr[pl.ds(j, 64, stride=CH), :] = t[:64]
        tr[pl.ds(j + 1, 64, stride=CH), :] = t[64:]

    for b in range(4):
        v1[pl.ds(b * 16, 16)] = tr[pl.ds(b * 384, 384), :].astype(BF16).reshape(16, CH, 128)

    pl.semaphore_wait(barrier, NG * GW - 1 + 3)

    here = x * 8 + z
    own_k = here * 2
    pltpu.make_async_copy(v1.at[me], r1.at[hf, x, yl, z], rcva.at[x]).start()
    pltpu.make_async_copy(v1.at[own_k + 1 - yl], b1.at[here], rcvb.at[x]).start()

    for i in range(NG):
        tx = lax.rem(x + i, NG)

        @pl.loop(1 if i == 0 else 0, 8)
        def _(n):
            tz = lax.rem(z + z_step(n), 8)
            k = tx * GW + tz * 2
            peer = k + yl
            send(v1.at[peer], r1.at[hf, x, yl, z], first.at[i], rcva.at[x], peer, hf)
            send(v1.at[k + 1 - yl], b1.at[here], first.at[i], rcvb.at[x], peer, hf)

        if i == 0:
            copy_m.wait()
        if i < 3:

            @pl.loop(12 * i, 12 * (i + 1))
            def _(n):
                b = n - 12 * i
                keep = mask_ref[hf * 3 + i, b].astype(F32)
                keep = jnp.full((TILE, TILE), keep, F32).astype(BF16)
                rows = pl.ds(i * TILE, TILE)
                cols = pl.ds(pl.multiple_of(b * TILE, TILE), TILE)
                for c in range(2):
                    mv[c, rows, cols] = mv[c, rows, cols] * keep

        if i >= 1:
            await_bytes(v1.at[pl.ds(0, 14 if i == 1 else 16)], first.at[i - 1])

    for table in tables[1:]:
        table.wait()
    acc[...] = jnp.zeros_like(acc)
    sign = jnp.where(low64, -1.0, 1.0).astype(F32)

    def slab(g):
        return pl.ds(g * 8, 8)

    def product(g, b):
        rows = pl.ds(pl.multiple_of(b * 192, 192), 192)
        cols = pl.ds(pl.multiple_of(g * 768, 768), 768)
        lhs = jnp.concatenate([mv[0, rows, cols], mv[1, rows, cols]], axis=0)
        return jnp.dot(lhs, fv[...], preferred_element_type=F32)

    @pl.loop(0, NG)
    def _(i):
        g = lax.rem(x - i + NG, NG)
        own = r1.at[hf, g, yl]
        await_bytes(own, rcva.at[g])
        send(own, own, snd.at[1], rel.at[0, g], me, ypeer)
        await_bytes(b1.at[slab(g)], rcvb.at[g])
        send(b1.at[slab(g)], own, snd.at[1], rel.at[1, g], beside, hf)
        send(b1.at[slab(g)], own, snd.at[1], rel.at[2, g], beside, ypeer)
        send(own, own, snd.at[2], chip.at[0, g], me, partner)

    @pl.loop(0, NG + 1)
    def _(i):
        @pl.when(i < NG)
        def _():
            g = lax.rem(x - i + NG, NG)
            for n, (h, y) in enumerate(((ypeer, yl), (hf, 1 - yl), (ypeer, 1 - yl))):
                got = r1.at[h, g, y]
                await_bytes(got, rel.at[n, g])
                send(got, got, snd.at[2], chip.at[n + 1, g], me, partner)

        @pl.when(i >= 1)
        def _():
            g = lax.rem(x - i + 1 + NG, NG)
            diag = (1 - yh) * 2 + (1 - q)
            for n, (h, y) in enumerate(
                ((partner, yl), (diag, yl), (partner, 1 - yl), (diag, 1 - yl))
            ):
                await_bytes(r1.at[h, g, y], chip.at[n, g])

            for t in range(2):
                for y in range(2):
                    b0 = r1[2 * t, g, y].astype(F32).reshape(192, 128)
                    b1_ = r1[2 * t + 1, g, y].astype(F32).reshape(192, 128)
                    o0 = jnp.where(low32, b0, pltpu.roll(b1_, 32, 1))
                    o1 = jnp.where(low32, pltpu.roll(b0, 96, 1), b1_)
                    for zz in range(8):
                        at = slice(zz * CH, (zz + 1) * CH)
                        rows = (zz * 2 + y) * 48
                        fv[rows : rows + 48, t * 128 : (t + 1) * 128] = jnp.concatenate(
                            [o0[at], o1[at]], axis=0
                        ).astype(BF16)

            @pl.when(i < NG)
            def _():
                @pl.loop(0, NG)
                def _(b):
                    acc[b] += product(g, b)

    @pl.loop(0, NG)
    def _(i):
        b = lax.rem(x + i, NG)
        full = acc[b] + product(lax.rem(x + 1, NG), b)
        for t in range(2):
            re = full[:192, t * 128 : (t + 1) * 128]
            im = full[192:, t * 128 : (t + 1) * 128]
            wv = re + sign * pltpu.roll(im, 64, 1)
            s2[t, pl.ds(b * 8, 8)] = wv.astype(BF16).reshape(8, CH, 128)

        @pl.loop(0, GW)
        def _(n):
            peer = wide_peer(me, i * GW + n)
            src = s2.at[lax.rem(peer, 2), lax.div(peer, 2)]

            @pl.when(i + n > 0)
            def _():
                send(src, r2.at[me], snd.at[3], rcv2, peer, hf)

            @pl.when(i + n == 0)
            def _():
                pltpu.make_async_copy(src, r2.at[me], rcv2).start()

    await_bytes(r2, rcv2)

    for b in range(4):
        big[pl.ds(b * 384, 384), :] = r2[pl.ds(b * 16, 16)].astype(F32).reshape(384, 128)
    points = jnp.broadcast_to(onset_ref[...], (8, 128))
    other = pltpu.roll(points, 64, 1)
    mine = jnp.where(
        yl == 0, jnp.where(low64, points, other), jnp.where(low64, other, points)
    )[0:1]
    mute = lax.broadcasted_iota(jnp.int32, (512, 128), 0) < mine
    mute = jnp.concatenate([mute, mute], axis=1)

    @pl.loop(0, 6, unroll=3)
    def _(rq):
        cols = []
        for u in range(2):
            r = rq * 4 + u * 2
            a0 = big[pl.ds(r, 64, stride=CH), :]
            a1 = big[pl.ds(r + 1, 64, stride=CH), :]
            top = jnp.where(low64, a0, pltpu.roll(a1, 64, 1))
            bot = jnp.where(low64, pltpu.roll(a0, 64, 1), a1)
            cols.append(jnp.concatenate([top, bot], axis=0))
        spec = jnp.concatenate(cols, axis=1).astype(BF16)
        trace = jnp.dot(invt_ref[...], spec, preferred_element_type=F32)
        muted = jnp.where(mute, trace, 0.0).astype(BF16)
        back = jnp.dot(fwdt_ref[...], muted, preferred_element_type=F32)
        for u in range(2):
            r = rq * 4 + u * 2
            top = back[:64, u * 128 : (u + 1) * 128]
            bot = back[64:, u * 128 : (u + 1) * 128]
            tr[pl.ds(r, 64, stride=CH), :] = jnp.where(low64, top, pltpu.roll(bot, 64, 1))
            tr[pl.ds(r + 1, 64, stride=CH), :] = jnp.where(low64, pltpu.roll(top, 64, 1), bot)

    for b in range(4):
        s3[pl.ds(b * 16, 16)] = tr[pl.ds(b * 384, 384), :].astype(BF16).reshape(16, CH, 128)
    slot = (lax.rem(me, 2), lax.div(me, 2))
    pltpu.make_async_copy(s3.at[me], h3.at[slot], rcv3).start()

    @pl.loop(1, NG * GW)
    def _(d):
        peer = wide_peer(me, d)
        send(s3.at[peer], h3.at[slot], snd.at[4], rcv3, peer, hf)

    await_bytes(h3, rcv3)

    for t in range(2):
        for b in range(2):
            piece = h3[t, pl.ds(b * 16, 16)].astype(F32).reshape(384, 128)
            for u in range(3):
                ht[t * 128 : (t + 1) * 128, b * 384 + u * 128 : b * 384 + (u + 1) * 128] = (
                    piece[u * 128 : (u + 1) * 128].T.astype(BF16)
                )

    @pl.loop(0, NG + 1)
    def _(i):
        @pl.when(i < NG)
        def _():
            g = lax.rem(x + i, NG)
            for b in range(3):
                cols = pl.ds(pl.multiple_of(g * 768 + b * TILE, TILE), TILE)
                pa = jnp.dot(ht[...], mv[0, :, cols], preferred_element_type=F32)
                pb = jnp.dot(ht[...], mv[1, :, cols], preferred_element_type=F32)
                pc = jnp.concatenate(
                    [
                        pa[0:64] + pb[64:128],
                        pa[64:128] - pb[0:64],
                        pa[128:192] + pb[192:256],
                        pa[192:256] - pb[128:192],
                    ],
                    axis=0,
                )
                pv[b * TILE : (b + 1) * TILE, :] = pc.T

            for t in range(2):
                for y in range(2):
                    i0, i1 = [
                        jnp.concatenate(
                            [
                                pv[
                                    (zz * 2 + y) * 48 + u * CH : (zz * 2 + y) * 48 + (u + 1) * CH,
                                    t * 128 : (t + 1) * 128,
                                ]
                                for zz in range(8)
                            ],
                            axis=0,
                        )
                        for u in range(2)
                    ]
                    o0 = jnp.where(low32, i0, pltpu.roll(i1, 32, 1)).astype(BF16)
                    o1 = jnp.where(low32, pltpu.roll(i0, 96, 1), i1).astype(BF16)
                    rs[2 * t, g, y] = o0.reshape(8, CH, 128)
                    rs[2 * t + 1, g, y] = o1.reshape(8, CH, 128)

            for t in range(2):
                send(rs.at[2 * t + (1 - q), g], qv.at[t, g], snd.at[5], rcvq.at[t, g], me, partner)

        @pl.when(i >= 1)
        def _():
            g = lax.rem(x + i - 1, NG)
            for t in range(2):
                await_bytes(qv.at[t, g], rcvq.at[t, g])
                total = rs[2 * t + q, g].astype(F32) + qv[t, g].astype(F32)
                zs[t, g] = total.astype(BF16)
            send(zs.at[1 - yh, g, 1 - yl], zr.at[2, g], snd.at[6], rcvz.at[2, g], beside, ypeer)
            send(zs.at[yh, g, 1 - yl], zr.at[1, g], snd.at[6], rcvz.at[1, g], beside, hf)
            send(zs.at[1 - yh, g, yl], zr.at[0, g], snd.at[6], rcvz.at[0, g], me, ypeer)

    @pl.loop(0, NG)
    def _(i):
        g = lax.rem(x + i, NG)
        for n in range(3):
            await_bytes(zr.at[n, g], rcvz.at[n, g])
        s4[yl, g] = (zs[yh, g, yl].astype(F32) + zr[0, g].astype(F32)).astype(BF16)
        s4[1 - yl, g] = (zr[1, g].astype(F32) + zr[2, g].astype(F32)).astype(BF16)

        @pl.loop(0, 8)
        def _(n):
            tz = lax.rem(z + z_step(n), 8)
            peer = g * GW + tz * 2 + yl
            k = x * GW + z * 2

            @pl.when(i + n > 0)
            def _():
                send(s4.at[0, g, tz], r4.at[k], snd.at[7], rcv4, peer, hf)
                send(s4.at[1, g, tz], r4.at[k + 1], snd.at[7], rcv4, peer, hf)

            @pl.when(i + n == 0)
            def _():
                pltpu.make_async_copy(s4.at[0, g, tz], r4.at[k], rcv4).start()
                pltpu.make_async_copy(s4.at[1, g, tz], r4.at[k + 1], rcv4).start()

    await_bytes(r4, rcv4)

    for b in range(4):
        big[pl.ds(b * 384, 384), :] = r4[pl.ds(b * 16, 16)].astype(F32).reshape(384, 128)

    @pl.loop(0, 12, unroll=4)
    def _(jp):
        j = 2 * jp
        a0 = big[pl.ds(j, 64, stride=CH), :]
        a1 = big[pl.ds(j + 1, 64, stride=CH), :]
        t = jnp.concatenate([a0, a1], axis=0).T
        l0 = jnp.where(low64, t[:64], pltpu.roll(t[64:], 64, 1))
        l1 = jnp.where(low64, pltpu.roll(t[:64], 64, 1), t[64:])
        for s in range(2):
            tr[pl.ds(s * CH + j, 32, stride=48), :] = l0[s * 32 : (s + 1) * 32]
            tr[pl.ds(s * CH + j + 1, 32, stride=48), :] = l1[s * 32 : (s + 1) * 32]

    time = lax.broadcasted_iota(jnp.int32, (48, 512), 1)
    for b in range(4):
        upd = jnp.dot(
            tr[pl.ds(b * 384, 384), :].astype(BF16), inv_ref[...], preferred_element_type=F32
        )
        for n in range(8):
            rows = pl.ds((b * 8 + n) * 48, 48)
            kept = jnp.where(time < onset_smem[hf * 32 + b * 8 + n], upd[n * 48 : (n + 1) * 48], 0.0)
            out_ref[rows, :] = (xv[rows, :].astype(F32) + kept).astype(BF16)

    n63 = pl.ds(0, NG * GW - 1)
    await_bytes(v1.at[pl.ds(0, 16)], first.at[NG - 1])
    await_bytes(rs.at[pl.ds(0, 3), :, 0], snd.at[1])
    await_bytes(rs.at[pl.ds(0, 2)], snd.at[2])
    await_bytes(r2.at[n63], snd.at[3])
    await_bytes(s3.at[n63], snd.at[4])
    await_bytes(rs.at[pl.ds(0, 2)], snd.at[5])
    await_bytes(zr, snd.at[6])
    await_bytes(r4.at[pl.ds(0, 62)], snd.at[7])


def focus_update(focus, kern, tile_mask, onset, points, fwd, fwdt, inv, invt):
    dma = pltpu.SemaphoreType.DMA
    vmem = pl.BlockSpec(memory_space=pltpu.VMEM)
    hbm = pl.BlockSpec(memory_space=pl.ANY)
    smem = pl.BlockSpec(memory_space=pltpu.SMEM)
    chunk = (CH, 128)
    return pl.pallas_call(
        focus_kernel,
        out_shape=pltpu.VMEM((1536, 512), BF16),
        in_specs=[hbm, hbm, smem, hbm, smem, hbm, hbm, hbm, hbm],
        out_specs=vmem,
        scratch_shapes=[
            pltpu.VMEM((1, 128), jnp.int32),
            pltpu.VMEM((512, 128), BF16),
            pltpu.VMEM((128, 512), BF16),
            pltpu.VMEM((128, 512), BF16),
            pltpu.VMEM((512, 128), BF16),
            pltpu.VMEM((1536, 512), BF16),
            pltpu.VMEM((2, 768, 3072), BF16),
            pltpu.VMEM((1536, 128), F32),
            pltpu.VMEM((1536, 128), F32),
            pltpu.VMEM((64, *chunk), BF16),
            pltpu.VMEM((32, *chunk), BF16),
            pltpu.VMEM((4, NG, 2, 8, *chunk), BF16),
            pltpu.VMEM((768, 256), BF16),
            pltpu.VMEM((NG, 384, 256), F32),
            pltpu.VMEM((2, 32, *chunk), BF16),
            pltpu.VMEM((64, *chunk), BF16),
            pltpu.VMEM((64, *chunk), BF16),
            pltpu.VMEM((2, 32, *chunk), BF16),
            pltpu.VMEM((256, 768), BF16),
            pltpu.VMEM((768, 256), F32),
            pltpu.VMEM((4, NG, 2, 8, *chunk), BF16),
            pltpu.VMEM((2, NG, 2, 8, *chunk), BF16),
            pltpu.VMEM((2, NG, 2, 8, *chunk), BF16),
            pltpu.VMEM((3, NG, 8, *chunk), BF16),
            pltpu.VMEM((2, NG, 8, *chunk), BF16),
            pltpu.VMEM((64, *chunk), BF16),
            dma((5,)), dma, dma, dma((8,)), dma((NG,)), dma((NG,)), dma((NG,)), dma((3, NG)), dma((4, NG)),
            dma, dma, dma((2, NG)), dma((3, NG)), dma,
        ],
        compiler_params=pltpu.CompilerParams(
            collective_id=0, has_side_effects=True, vmem_limit_bytes=50 * 1024 * 1024
        ),
        name="focus_update",
    )(focus, kern, tile_mask, onset, points, fwd, fwdt, inv, invt)


def shards(focus, kernel, onset, tile_mask):
    own_points, local_receivers, length = focus.shape
    fwd, fwdt, inv, invt = make_tables(64, length)
    pinned = functools.partial(pltpu.with_memory_space_constraint, memory_space=pltpu.HBM)
    out = focus_update(
        pinned(focus.reshape(own_points * local_receivers, length)),
        pinned(kernel[0]), pinned(tile_mask), pinned(onset.reshape(1, 128)), onset, *map(pinned, (fwd, fwdt, inv, invt)),
    )
    return out.reshape(focus.shape)


def solution(mesh):
    in_specs = (P("half", "wide", None), P("wide", None, "half", None), P(), P())
    out_specs = P("half", "wide", None)
    return jax.shard_map(shards, mesh=mesh, in_specs=in_specs, out_specs=out_specs, check_vma=False)
```

```python
import functools

import jax
import jax.numpy as jnp
import numpy as np
from jax import lax
from jax.experimental import pallas as pl
from jax.experimental.pallas import tpu as pltpu
from jax.sharding import PartitionSpec as P

TILE = 256
NG = 4
GW = 16
CH = 24
F32 = jnp.float32
BF16 = jnp.bfloat16


def make_tables(bins, length):
    k = np.arange(1, bins + 1)
    t = np.arange(length)
    phase = (t[:, None] * k[None, :] % length).astype(np.float32) * np.float32(
        2.0 * np.pi / length
    )
    table = np.concatenate([np.cos(phase), -np.sin(phase)], axis=1)
    fwd = jnp.asarray(table, F32).astype(BF16)
    invt = jnp.asarray(table * (2.0 / length), F32).astype(BF16)
    return fwd, fwd.T, invt.T, invt


def z_step(n):
    m = lax.div(n, 2)
    return jnp.where(n < 2, 4 * n, jnp.where(lax.rem(n, 2) == 0, m, 8 - m))


def wide_peer(me, d):
    x, loc = lax.div(me, GW), lax.rem(me, GW)
    i, n = lax.div(d, GW), lax.rem(d, GW)
    z, y = lax.div(loc, 2), lax.rem(loc, 2)
    tx = lax.rem(x + i, NG)
    tz = lax.rem(z + z_step(lax.div(n, 2)), 8)
    ty = lax.rem(y + lax.rem(n, 2), 2)
    return tx * GW + tz * 2 + ty


def send(src, dst, ssem, rsem, wide, half):
    pltpu.make_async_remote_copy(
        src_ref=src,
        dst_ref=dst,
        send_sem=ssem,
        recv_sem=rsem,
        device_id={"wide": wide, "half": half},
        device_id_type=pl.DeviceIdType.MESH,
    ).start()


def await_bytes(ref, sem):
    pltpu.make_async_copy(ref, ref, sem).wait()


def focus_kernel(
    focus_hbm, kern_hbm, mask_ref, onset_hbm, onset_smem, fwd_hbm, fwdt_hbm, inv_hbm, invt_hbm,
    out_ref,
    onset_ref, fwd_ref, fwdt_ref, inv_ref, invt_ref, xv, mv, big, tr, v1, b1, r1, fv, acc, s2a, s2b, r2a, r2b, s3a, s3b, h3a, h3b, ht, pv, rs, qv, zs, zr, s4, r4,
    sem_t, sem_x, sem_m, snd, first, rcva, rcvb, rel, chip, rcv2, rcv3, rcvq, rcvz, rcv4,
):
    me = lax.axis_index("wide")
    hf = lax.axis_index("half")
    x = lax.div(me, GW)
    yh, q = lax.div(hf, 2), lax.rem(hf, 2)
    partner = yh * 2 + (1 - q)
    ypeer = (1 - yh) * 2 + q
    z, yl = lax.div(lax.rem(me, GW), 2), lax.rem(me, 2)
    beside = x * GW + 2 * z + (1 - yl)
    barrier = pltpu.get_barrier_semaphore()

    @pl.loop(1, NG * GW)
    def _(d):
        pl.semaphore_signal(
            barrier,
            inc=1,
            device_id={"wide": wide_peer(me, d), "half": hf},
            device_id_type=pl.DeviceIdType.MESH,
        )

    for w, other in ((me, partner), (me, ypeer), (beside, ypeer)):
        pl.semaphore_signal(
            barrier,
            inc=1,
            device_id={"wide": w, "half": other},
            device_id_type=pl.DeviceIdType.MESH,
        )

    tables = [
        pltpu.make_async_copy(src, dst, sem_t.at[n])
        for n, (src, dst) in enumerate(
            (
                (fwd_hbm, fwd_ref), (fwdt_hbm, fwdt_ref), (inv_hbm, inv_ref),
                (invt_hbm, invt_ref), (onset_hbm, onset_ref),
            )
        )
    ]
    tables[0].start()
    copy_x = pltpu.make_async_copy(focus_hbm, xv, sem_x)
    copy_x.start()
    copy_m = pltpu.make_async_copy(kern_hbm, mv, sem_m)
    copy_m.start()
    for table in tables[1:]:
        table.start()

    lane = lax.broadcasted_iota(jnp.int32, (1, 128), 1)
    low64 = lane < 64
    low32 = lax.rem(lane, 64) < 32

    tables[0].wait()
    copy_x.wait()
    for b in range(4):
        rows = pl.ds(b * 384, 384)
        big[rows, :] = jnp.dot(xv[rows, :], fwd_ref[...], preferred_element_type=F32)

    @pl.loop(0, 12, unroll=4)
    def _(jp):
        j = 2 * jp
        a = [
            [big[pl.ds(s * CH + j + jj, 32, stride=48), :] for jj in range(2)]
            for s in range(2)
        ]
        even = [jnp.where(low64, a[s][0], pltpu.roll(a[s][1], 64, 1)) for s in range(2)]
        odd = [jnp.where(low64, pltpu.roll(a[s][0], 64, 1), a[s][1]) for s in range(2)]
        t = jnp.concatenate(even + odd, axis=0).T
        tr[pl.ds(j, 64, stride=CH), :] = t[:64]
        tr[pl.ds(j + 1, 64, stride=CH), :] = t[64:]

    for b in range(4):
        v1[pl.ds(b * 16, 16)] = tr[pl.ds(b * 384, 384), :].astype(BF16).reshape(16, CH, 128)

    pl.semaphore_wait(barrier, NG * GW - 1 + 3)

    here = x * 8 + z
    own_k = here * 2
    pltpu.make_async_copy(v1.at[me], r1.at[hf, x, yl, z], rcva.at[x]).start()
    pltpu.make_async_copy(v1.at[own_k + 1 - yl], b1.at[here], rcvb.at[x]).start()

    for i in range(NG):
        tx = lax.rem(x + i, NG)

        @pl.loop(1 if i == 0 else 0, 8)
        def _(n):
            tz = lax.rem(z + z_step(n), 8)
            k = tx * GW + tz * 2
            peer = k + yl
            send(v1.at[peer], r1.at[hf, x, yl, z], first.at[i], rcva.at[x], peer, hf)
            send(v1.at[k + 1 - yl], b1.at[here], first.at[i], rcvb.at[x], peer, hf)

        if i == 0:
            copy_m.wait()
        if i < 3:

            @pl.loop(12 * i, 12 * (i + 1))
            def _(n):
                b = n - 12 * i
                keep = mask_ref[hf * 3 + i, b].astype(F32)
                keep = jnp.full((TILE, TILE), keep, F32).astype(BF16)
                rows = pl.ds(i * TILE, TILE)
                cols = pl.ds(pl.multiple_of(b * TILE, TILE), TILE)
                for c in range(2):
                    mv[c, rows, cols] = mv[c, rows, cols] * keep

        if i >= 1:
            await_bytes(v1.at[pl.ds(0, 14 if i == 1 else 16)], first.at[i - 1])

    for table in tables[1:]:
        table.wait()
    acc[...] = jnp.zeros_like(acc)
    sign = jnp.where(low64, -1.0, 1.0).astype(F32)

    def slab(g):
        return pl.ds(g * 8, 8)

    def product(g, b):
        rows = pl.ds(pl.multiple_of(b * TILE, TILE), TILE)
        cols = pl.ds(pl.multiple_of(g * 768, 768), 768)
        lhs = jnp.concatenate([mv[0, rows, cols], mv[1, rows, cols]], axis=0)
        return jnp.dot(lhs, fv[...], preferred_element_type=F32)

    @pl.loop(0, NG)
    def _(i):
        g = lax.rem(x - i + NG, NG)
        own = r1.at[hf, g, yl]
        await_bytes(own, rcva.at[g])
        send(own, own, snd.at[1], rel.at[0, g], me, ypeer)
        await_bytes(b1.at[slab(g)], rcvb.at[g])
        send(b1.at[slab(g)], own, snd.at[1], rel.at[1, g], beside, hf)
        send(b1.at[slab(g)], own, snd.at[1], rel.at[2, g], beside, ypeer)
        send(own, own, snd.at[2], chip.at[0, g], me, partner)

    @pl.loop(0, NG + 1)
    def _(i):
        @pl.when(i < NG)
        def _():
            g = lax.rem(x - i + NG, NG)
            for n, (h, y) in enumerate(((ypeer, yl), (hf, 1 - yl), (ypeer, 1 - yl))):
                got = r1.at[h, g, y]
                await_bytes(got, rel.at[n, g])
                send(got, got, snd.at[2], chip.at[n + 1, g], me, partner)

        @pl.when(i >= 1)
        def _():
            g = lax.rem(x - i + 1 + NG, NG)
            diag = (1 - yh) * 2 + (1 - q)
            for n, (h, y) in enumerate(
                ((partner, yl), (diag, yl), (partner, 1 - yl), (diag, 1 - yl))
            ):
                await_bytes(r1.at[h, g, y], chip.at[n, g])

            for t in range(2):
                for y in range(2):
                    b0 = r1[2 * t, g, y].astype(F32).reshape(192, 128)
                    b1_ = r1[2 * t + 1, g, y].astype(F32).reshape(192, 128)
                    o0 = jnp.where(low32, b0, pltpu.roll(b1_, 32, 1))
                    o1 = jnp.where(low32, pltpu.roll(b0, 96, 1), b1_)
                    for zz in range(8):
                        at = slice(zz * CH, (zz + 1) * CH)
                        rows = (zz * 2 + y) * 48
                        fv[rows : rows + 48, t * 128 : (t + 1) * 128] = jnp.concatenate(
                            [o0[at], o1[at]], axis=0
                        ).astype(BF16)

            @pl.when(i < NG)
            def _():
                @pl.loop(0, 3)
                def _(b):
                    acc[b] += product(g, b)

    def waves(b):
        full = acc[b] + product(lax.rem(x + 1, NG), b)
        return [
            (
                full[:TILE, t * 128 : (t + 1) * 128]
                + sign * pltpu.roll(full[TILE:, t * 128 : (t + 1) * 128], 64, 1)
            ).astype(BF16)
            for t in range(2)
        ]

    def spread(first, last, src_of, dst, ssem, rsem):
        @pl.loop(first, last)
        def _(d):
            peer = wide_peer(me, d)

            @pl.when(d > 0)
            def _():
                send(src_of(peer), dst, ssem, rsem, peer, hf)

            @pl.when(d == 0)
            def _():
                pltpu.make_async_copy(src_of(peer), dst, rsem).start()

    def by_row(ref):
        return lambda peer: ref.at[lax.rem(peer, 2), lax.div(peer, 2)]

    @pl.loop(0, 2)
    def _(i):
        b = lax.rem(lax.div(x, 2) + i, 2)
        for t, wv in enumerate(waves(b)):
            s2a[t, pl.ds(b * 16, 16)] = wv.reshape(16, 16, 128)

        @pl.loop(0, 32)
        def _(n):
            tx = 2 * b + lax.rem(lax.rem(x, 2) + lax.div(n, GW), 2)
            peer = tx * GW + lax.rem(wide_peer(me, n), GW)

            @pl.when(i + n > 0)
            def _():
                send(by_row(s2a)(peer), r2a.at[me], snd.at[3], rcv2.at[0], peer, hf)

            @pl.when(i + n == 0)
            def _():
                pltpu.make_async_copy(by_row(s2a)(peer), r2a.at[me], rcv2.at[0]).start()

    for t, wv in enumerate(waves(2)):
        s2b[t] = wv.reshape(32, 8, 128)
    n63 = pl.ds(0, NG * GW - 1)
    await_bytes(r2a.at[n63], snd.at[3])
    spread(0, NG * GW, by_row(s2b), r2b.at[me], snd.at[8], rcv2.at[1])

    points = jnp.broadcast_to(onset_ref[...], (8, 128))
    other = pltpu.roll(points, 64, 1)
    mine = jnp.where(
        yl == 0, jnp.where(low64, points, other), jnp.where(low64, other, points)
    )[0:1]
    mute = lax.broadcasted_iota(jnp.int32, (512, 128), 0) < mine
    mute = jnp.concatenate([mute, mute], axis=1)

    def time_domain(base, count):
        @pl.loop(0, count // 4, unroll=2)
        def _(rq):
            time_step(base + rq * 4, count)

    def time_step(base, count):
        cols = []
        for u in range(2):
            r = base + u * 2
            a0 = big[pl.ds(r, 64, stride=count), :]
            a1 = big[pl.ds(r + 1, 64, stride=count), :]
            top = jnp.where(low64, a0, pltpu.roll(a1, 64, 1))
            bot = jnp.where(low64, pltpu.roll(a0, 64, 1), a1)
            cols.append(jnp.concatenate([top, bot], axis=0))
        spec = jnp.concatenate(cols, axis=1).astype(BF16)
        trace = jnp.dot(invt_ref[...], spec, preferred_element_type=F32)
        muted = jnp.where(mute, trace, 0.0).astype(BF16)
        back = jnp.dot(fwdt_ref[...], muted, preferred_element_type=F32)
        for u in range(2):
            r = base + u * 2
            top = back[:64, u * 128 : (u + 1) * 128]
            bot = back[64:, u * 128 : (u + 1) * 128]
            tr[pl.ds(r, 64, stride=count), :] = jnp.where(low64, top, pltpu.roll(bot, 64, 1))
            tr[pl.ds(r + 1, 64, stride=count), :] = jnp.where(low64, pltpu.roll(top, 64, 1), bot)

    slot = (lax.rem(me, 2), lax.div(me, 2))
    await_bytes(r2a, rcv2.at[0])
    big[0:1024, :] = r2a[...].astype(F32).reshape(1024, 128)
    time_domain(0, 16)
    s3a[...] = tr[0:1024, :].astype(BF16).reshape(64, 16, 128)
    spread(0, NG * GW, lambda peer: s3a.at[peer], h3a.at[slot], snd.at[4], rcv3.at[0])
    await_bytes(r2b, rcv2.at[1])
    big[1024:1536, :] = r2b[...].astype(F32).reshape(512, 128)
    time_domain(1024, 8)
    s3b[...] = tr[1024:1536, :].astype(BF16).reshape(64, 8, 128)
    spread(0, NG * GW, lambda peer: s3b.at[peer], h3b.at[slot], snd.at[9], rcv3.at[1])

    await_bytes(h3a, rcv3.at[0])
    for t in range(2):
        for u in range(4):
            piece = h3a[t, pl.ds(u * 8, 8)].astype(F32).reshape(128, 128)
            ht[t * 128 : (t + 1) * 128, u * 128 : (u + 1) * 128] = piece.T.astype(BF16)
    await_bytes(h3b, rcv3.at[1])
    for t in range(2):
        for u in range(2):
            piece = h3b[t, pl.ds(u * 16, 16)].astype(F32).reshape(128, 128)
            ht[t * 128 : (t + 1) * 128, 512 + u * 128 : 512 + (u + 1) * 128] = piece.T.astype(BF16)

    @pl.loop(0, NG + 1)
    def _(i):
        @pl.when(i < NG)
        def _():
            g = lax.rem(x + i, NG)
            for b in range(3):
                cols = pl.ds(pl.multiple_of(g * 768 + b * TILE, TILE), TILE)
                pa = jnp.dot(ht[...], mv[0, :, cols], preferred_element_type=F32)
                pb = jnp.dot(ht[...], mv[1, :, cols], preferred_element_type=F32)
                pc = jnp.concatenate(
                    [
                        pa[0:64] + pb[64:128],
                        pa[64:128] - pb[0:64],
                        pa[128:192] + pb[192:256],
                        pa[192:256] - pb[128:192],
                    ],
                    axis=0,
                )
                pv[b * TILE : (b + 1) * TILE, :] = pc.T

            for t in range(2):
                for y in range(2):
                    i0, i1 = [
                        jnp.concatenate(
                            [
                                pv[
                                    (zz * 2 + y) * 48 + u * CH : (zz * 2 + y) * 48 + (u + 1) * CH,
                                    t * 128 : (t + 1) * 128,
                                ]
                                for zz in range(8)
                            ],
                            axis=0,
                        )
                        for u in range(2)
                    ]
                    o0 = jnp.where(low32, i0, pltpu.roll(i1, 32, 1)).astype(BF16)
                    o1 = jnp.where(low32, pltpu.roll(i0, 96, 1), i1).astype(BF16)
                    rs[2 * t, g, y] = o0.reshape(8, CH, 128)
                    rs[2 * t + 1, g, y] = o1.reshape(8, CH, 128)

            for t in range(2):
                send(rs.at[2 * t + (1 - q), g], qv.at[t, g], snd.at[5], rcvq.at[t, g], me, partner)

        @pl.when(i >= 1)
        def _():
            g = lax.rem(x + i - 1, NG)
            for t in range(2):
                await_bytes(qv.at[t, g], rcvq.at[t, g])
                total = rs[2 * t + q, g].astype(F32) + qv[t, g].astype(F32)
                zs[t, g] = total.astype(BF16)
            send(zs.at[1 - yh, g, 1 - yl], zr.at[2, g], snd.at[6], rcvz.at[2, g], beside, ypeer)
            send(zs.at[yh, g, 1 - yl], zr.at[1, g], snd.at[6], rcvz.at[1, g], beside, hf)
            send(zs.at[1 - yh, g, yl], zr.at[0, g], snd.at[6], rcvz.at[0, g], me, ypeer)

    @pl.loop(0, NG)
    def _(i):
        g = lax.rem(x + i, NG)
        for n in range(3):
            await_bytes(zr.at[n, g], rcvz.at[n, g])
        s4[yl, g] = (zs[yh, g, yl].astype(F32) + zr[0, g].astype(F32)).astype(BF16)
        s4[1 - yl, g] = (zr[1, g].astype(F32) + zr[2, g].astype(F32)).astype(BF16)

        @pl.loop(0, 8)
        def _(n):
            tz = lax.rem(z + z_step(n), 8)
            peer = g * GW + tz * 2 + yl
            k = x * GW + z * 2

            @pl.when(i + n > 0)
            def _():
                send(s4.at[0, g, tz], r4.at[k], snd.at[7], rcv4, peer, hf)
                send(s4.at[1, g, tz], r4.at[k + 1], snd.at[7], rcv4, peer, hf)

            @pl.when(i + n == 0)
            def _():
                pltpu.make_async_copy(s4.at[0, g, tz], r4.at[k], rcv4).start()
                pltpu.make_async_copy(s4.at[1, g, tz], r4.at[k + 1], rcv4).start()

    await_bytes(r4, rcv4)

    for b in range(4):
        big[pl.ds(b * 384, 384), :] = r4[pl.ds(b * 16, 16)].astype(F32).reshape(384, 128)

    @pl.loop(0, 12, unroll=4)
    def _(jp):
        j = 2 * jp
        a0 = big[pl.ds(j, 64, stride=CH), :]
        a1 = big[pl.ds(j + 1, 64, stride=CH), :]
        t = jnp.concatenate([a0, a1], axis=0).T
        l0 = jnp.where(low64, t[:64], pltpu.roll(t[64:], 64, 1))
        l1 = jnp.where(low64, pltpu.roll(t[:64], 64, 1), t[64:])
        for s in range(2):
            tr[pl.ds(s * CH + j, 32, stride=48), :] = l0[s * 32 : (s + 1) * 32]
            tr[pl.ds(s * CH + j + 1, 32, stride=48), :] = l1[s * 32 : (s + 1) * 32]

    time = lax.broadcasted_iota(jnp.int32, (48, 512), 1)
    for b in range(4):
        upd = jnp.dot(
            tr[pl.ds(b * 384, 384), :].astype(BF16), inv_ref[...], preferred_element_type=F32
        )
        for n in range(8):
            rows = pl.ds((b * 8 + n) * 48, 48)
            kept = jnp.where(time < onset_smem[hf * 32 + b * 8 + n], upd[n * 48 : (n + 1) * 48], 0.0)
            out_ref[rows, :] = (xv[rows, :].astype(F32) + kept).astype(BF16)

    await_bytes(v1.at[pl.ds(0, 16)], first.at[NG - 1])
    await_bytes(rs.at[pl.ds(0, 3), :, 0], snd.at[1])
    await_bytes(rs.at[pl.ds(0, 2)], snd.at[2])
    await_bytes(s3a.at[n63], snd.at[4])
    await_bytes(s3b.at[n63], snd.at[8])
    await_bytes(s3b.at[n63], snd.at[9])
    await_bytes(rs.at[pl.ds(0, 2)], snd.at[5])
    await_bytes(zr, snd.at[6])
    await_bytes(r4.at[pl.ds(0, 62)], snd.at[7])


def focus_update(focus, kern, tile_mask, onset, points, fwd, fwdt, inv, invt):
    dma = pltpu.SemaphoreType.DMA
    vmem = pl.BlockSpec(memory_space=pltpu.VMEM)
    hbm = pl.BlockSpec(memory_space=pl.ANY)
    smem = pl.BlockSpec(memory_space=pltpu.SMEM)
    chunk = (CH, 128)
    return pl.pallas_call(
        focus_kernel,
        out_shape=pltpu.VMEM((1536, 512), BF16),
        in_specs=[hbm, hbm, smem, hbm, smem, hbm, hbm, hbm, hbm],
        out_specs=vmem,
        scratch_shapes=[
            pltpu.VMEM((1, 128), jnp.int32),
            pltpu.VMEM((512, 128), BF16),
            pltpu.VMEM((128, 512), BF16),
            pltpu.VMEM((128, 512), BF16),
            pltpu.VMEM((512, 128), BF16),
            pltpu.VMEM((1536, 512), BF16),
            pltpu.VMEM((2, 768, 3072), BF16),
            pltpu.VMEM((1536, 128), F32),
            pltpu.VMEM((1536, 128), F32),
            pltpu.VMEM((64, *chunk), BF16),
            pltpu.VMEM((32, *chunk), BF16),
            pltpu.VMEM((4, NG, 2, 8, *chunk), BF16),
            pltpu.VMEM((768, 256), BF16),
            pltpu.VMEM((3, 512, 256), F32),
            pltpu.VMEM((2, 32, 16, 128), BF16),
            pltpu.VMEM((2, 32, 8, 128), BF16),
            pltpu.VMEM((64, 16, 128), BF16),
            pltpu.VMEM((64, 8, 128), BF16),
            pltpu.VMEM((64, 16, 128), BF16),
            pltpu.VMEM((64, 8, 128), BF16),
            pltpu.VMEM((2, 32, 16, 128), BF16),
            pltpu.VMEM((2, 32, 8, 128), BF16),
            pltpu.VMEM((256, 768), BF16),
            pltpu.VMEM((768, 256), F32),
            pltpu.VMEM((4, NG, 2, 8, *chunk), BF16),
            pltpu.VMEM((2, NG, 2, 8, *chunk), BF16),
            pltpu.VMEM((2, NG, 2, 8, *chunk), BF16),
            pltpu.VMEM((3, NG, 8, *chunk), BF16),
            pltpu.VMEM((2, NG, 8, *chunk), BF16),
            pltpu.VMEM((64, *chunk), BF16),
            dma((5,)), dma, dma, dma((10,)), dma((NG,)), dma((NG,)), dma((NG,)), dma((3, NG)), dma((4, NG)),
            dma((2,)), dma((2,)), dma((2, NG)), dma((3, NG)), dma,
        ],
        compiler_params=pltpu.CompilerParams(
            collective_id=0, has_side_effects=True, vmem_limit_bytes=50 * 1024 * 1024
        ),
        name="focus_update",
    )(focus, kern, tile_mask, onset, points, fwd, fwdt, inv, invt)


def shards(focus, kernel, onset, tile_mask):
    own_points, local_receivers, length = focus.shape
    fwd, fwdt, inv, invt = make_tables(64, length)
    pinned = functools.partial(pltpu.with_memory_space_constraint, memory_space=pltpu.HBM)
    out = focus_update(
        pinned(focus.reshape(own_points * local_receivers, length)),
        pinned(kernel[0]), pinned(tile_mask), pinned(onset.reshape(1, 128)), onset, *map(pinned, (fwd, fwdt, inv, invt)),
    )
    return out.reshape(focus.shape)


def solution(mesh):
    in_specs = (P("half", "wide", None), P("wide", None, "half", None), P(), P())
    out_specs = P("half", "wide", None)
    return jax.shard_map(shards, mesh=mesh, in_specs=in_specs, out_specs=out_specs, check_vma=False)
```

```python
import functools

import jax
import jax.numpy as jnp
import numpy as np
from jax import lax
from jax.experimental import pallas as pl
from jax.experimental.pallas import tpu as pltpu
from jax.sharding import PartitionSpec as P

TILE = 256
NG = 4
GW = 16
CH = 24
F32 = jnp.float32
BF16 = jnp.bfloat16


def make_tables(bins, length):
    k = np.arange(1, bins + 1)
    t = np.arange(length)
    phase = (t[:, None] * k[None, :] % length).astype(np.float32) * np.float32(
        2.0 * np.pi / length
    )
    table = np.concatenate([np.cos(phase), -np.sin(phase)], axis=1)
    fwd = jnp.asarray(table, F32).astype(BF16)
    invt = jnp.asarray(table * (2.0 / length), F32).astype(BF16)
    return fwd, fwd.T, invt.T, invt


def z_step(n):
    m = lax.div(n, 2)
    return jnp.where(n < 2, 4 * n, jnp.where(lax.rem(n, 2) == 0, m, 8 - m))


def wide_peer(me, d):
    x, loc = lax.div(me, GW), lax.rem(me, GW)
    i, n = lax.div(d, GW), lax.rem(d, GW)
    z, y = lax.div(loc, 2), lax.rem(loc, 2)
    tx = lax.rem(x + i, NG)
    tz = lax.rem(z + z_step(lax.div(n, 2)), 8)
    ty = lax.rem(y + lax.rem(n, 2), 2)
    return tx * GW + tz * 2 + ty


def send(src, dst, ssem, rsem, wide, half):
    pltpu.make_async_remote_copy(
        src_ref=src,
        dst_ref=dst,
        send_sem=ssem,
        recv_sem=rsem,
        device_id={"wide": wide, "half": half},
        device_id_type=pl.DeviceIdType.MESH,
    ).start()


def await_bytes(ref, sem):
    pltpu.make_async_copy(ref, ref, sem).wait()


def focus_kernel(
    focus_hbm, kern_hbm, mask_ref, onset_hbm, onset_smem, fwd_hbm, fwdt_hbm, inv_hbm, invt_hbm,
    out_ref,
    onset_ref, fwd_ref, fwdt_ref, inv_ref, invt_ref, xv, mv, big, tr, v1, b1, r1, fv, acc, s2, r2, s3, h3, ht, pv, rs, qv, zs, zr, s4, r4,
    sem_t, sem_x, sem_m, snd, first, away, back, rcva, rcvb, rel, chip, rcv2, rcv3, rcvq, rcvz, rcv4,
):
    me = lax.axis_index("wide")
    hf = lax.axis_index("half")
    x = lax.div(me, GW)
    yh, q = lax.div(hf, 2), lax.rem(hf, 2)
    partner = yh * 2 + (1 - q)
    ypeer = (1 - yh) * 2 + q
    z, yl = lax.div(lax.rem(me, GW), 2), lax.rem(me, 2)
    beside = x * GW + 2 * z + (1 - yl)
    barrier = pltpu.get_barrier_semaphore()

    @pl.loop(1, NG * GW)
    def _(d):
        pl.semaphore_signal(
            barrier,
            inc=1,
            device_id={"wide": wide_peer(me, d), "half": hf},
            device_id_type=pl.DeviceIdType.MESH,
        )

    for w, other in ((me, partner), (me, ypeer), (beside, ypeer)):
        pl.semaphore_signal(
            barrier,
            inc=1,
            device_id={"wide": w, "half": other},
            device_id_type=pl.DeviceIdType.MESH,
        )

    tables = [
        pltpu.make_async_copy(src, dst, sem_t.at[n])
        for n, (src, dst) in enumerate(
            (
                (fwd_hbm, fwd_ref), (fwdt_hbm, fwdt_ref), (inv_hbm, inv_ref),
                (invt_hbm, invt_ref), (onset_hbm, onset_ref),
            )
        )
    ]
    tables[0].start()
    copy_x = pltpu.make_async_copy(focus_hbm, xv, sem_x)
    copy_x.start()
    copy_m = pltpu.make_async_copy(kern_hbm, mv, sem_m)
    copy_m.start()
    for table in tables[1:]:
        table.start()

    lane = lax.broadcasted_iota(jnp.int32, (1, 128), 1)
    low64 = lane < 64
    low32 = lax.rem(lane, 64) < 32

    tables[0].wait()
    copy_x.wait()
    for b in range(4):
        rows = pl.ds(b * 384, 384)
        big[rows, :] = jnp.dot(xv[rows, :], fwd_ref[...], preferred_element_type=F32)

    @pl.loop(0, 12, unroll=4)
    def _(jp):
        j = 2 * jp
        a = [
            [big[pl.ds(s * CH + j + jj, 32, stride=48), :] for jj in range(2)]
            for s in range(2)
        ]
        even = [jnp.where(low64, a[s][0], pltpu.roll(a[s][1], 64, 1)) for s in range(2)]
        odd = [jnp.where(low64, pltpu.roll(a[s][0], 64, 1), a[s][1]) for s in range(2)]
        t = jnp.concatenate(even + odd, axis=0).T
        tr[pl.ds(j, 64, stride=CH), :] = t[:64]
        tr[pl.ds(j + 1, 64, stride=CH), :] = t[64:]

    for b in range(4):
        v1[pl.ds(b * 16, 16)] = tr[pl.ds(b * 384, 384), :].astype(BF16).reshape(16, CH, 128)

    pl.semaphore_wait(barrier, NG * GW - 1 + 3)

    here = x * 8 + z
    own_k = here * 2
    pltpu.make_async_copy(v1.at[me], r1.at[hf, x, yl, z], rcva.at[x]).start()
    pltpu.make_async_copy(v1.at[own_k + 1 - yl], b1.at[here], rcvb.at[x]).start()

    for i in range(NG):
        tx = lax.rem(x + i, NG)

        @pl.loop(1 if i == 0 else 0, 8)
        def _(n):
            tz = lax.rem(z + z_step(n), 8)
            k = tx * GW + tz * 2
            peer = k + yl
            send(v1.at[peer], r1.at[hf, x, yl, z], first.at[i], rcva.at[x], peer, hf)
            send(v1.at[k + 1 - yl], b1.at[here], first.at[i], rcvb.at[x], peer, hf)

        if i == 0:
            copy_m.wait()
        if i < 3:

            @pl.loop(12 * i, 12 * (i + 1))
            def _(n):
                b = n - 12 * i
                keep = mask_ref[hf * 3 + i, b].astype(F32)
                keep = jnp.full((TILE, TILE), keep, F32).astype(BF16)
                rows = pl.ds(i * TILE, TILE)
                cols = pl.ds(pl.multiple_of(b * TILE, TILE), TILE)
                for c in range(2):
                    mv[c, rows, cols] = mv[c, rows, cols] * keep

        if i >= 1:
            await_bytes(v1.at[pl.ds(0, 14 if i == 1 else 16)], first.at[i - 1])

    for table in tables[1:]:
        table.wait()
    acc[...] = jnp.zeros_like(acc)
    sign = jnp.where(low64, -1.0, 1.0).astype(F32)

    def slab(g):
        return pl.ds(g * 8, 8)

    def product(g, b):
        rows = pl.ds(pl.multiple_of(b * TILE, TILE), TILE)
        cols = pl.ds(pl.multiple_of(g * 768, 768), 768)
        lhs = jnp.concatenate([mv[0, rows, cols], mv[1, rows, cols]], axis=0)
        return jnp.dot(lhs, fv[...], preferred_element_type=F32)

    @pl.loop(0, NG)
    def _(i):
        g = lax.rem(x - i + NG, NG)
        own = r1.at[hf, g, yl]
        await_bytes(own, rcva.at[g])
        send(own, own, snd.at[1], rel.at[0, g], me, ypeer)
        await_bytes(b1.at[slab(g)], rcvb.at[g])
        send(b1.at[slab(g)], own, snd.at[1], rel.at[1, g], beside, hf)
        send(b1.at[slab(g)], own, snd.at[1], rel.at[2, g], beside, ypeer)
        send(own, own, snd.at[2], chip.at[0, g], me, partner)

    @pl.loop(0, NG + 1)
    def _(i):
        @pl.when(i < NG)
        def _():
            g = lax.rem(x - i + NG, NG)
            for n, (h, y) in enumerate(((ypeer, yl), (hf, 1 - yl), (ypeer, 1 - yl))):
                got = r1.at[h, g, y]
                await_bytes(got, rel.at[n, g])
                send(got, got, snd.at[2], chip.at[n + 1, g], me, partner)

        @pl.when(i >= 1)
        def _():
            g = lax.rem(x - i + 1 + NG, NG)
            diag = (1 - yh) * 2 + (1 - q)
            for n, (h, y) in enumerate(
                ((partner, yl), (diag, yl), (partner, 1 - yl), (diag, 1 - yl))
            ):
                await_bytes(r1.at[h, g, y], chip.at[n, g])

            for t in range(2):
                for y in range(2):
                    b0 = r1[2 * t, g, y].astype(F32).reshape(192, 128)
                    b1_ = r1[2 * t + 1, g, y].astype(F32).reshape(192, 128)
                    o0 = jnp.where(low32, b0, pltpu.roll(b1_, 32, 1))
                    o1 = jnp.where(low32, pltpu.roll(b0, 96, 1), b1_)
                    for zz in range(8):
                        at = slice(zz * CH, (zz + 1) * CH)
                        rows = (zz * 2 + y) * 48
                        fv[rows : rows + 48, t * 128 : (t + 1) * 128] = jnp.concatenate(
                            [o0[at], o1[at]], axis=0
                        ).astype(BF16)

            @pl.when(i < NG)
            def _():
                @pl.loop(0, 3)
                def _(b):
                    acc[b] += product(g, b)

    def waves(b):
        full = acc[b] + product(lax.rem(x + 1, NG), b)
        return [
            (
                full[:TILE, t * 128 : (t + 1) * 128]
                + sign * pltpu.roll(full[TILE:, t * 128 : (t + 1) * 128], 64, 1)
            ).astype(BF16)
            for t in range(2)
        ]

    def spread(first, last, src_of, dst, ssem, rsem):
        @pl.loop(first, last)
        def _(d):
            peer = wide_peer(me, d)

            @pl.when(d > 0)
            def _():
                send(src_of(peer), dst, ssem, rsem, peer, hf)

            @pl.when(d == 0)
            def _():
                pltpu.make_async_copy(src_of(peer), dst, rsem).start()

    def by_row(ref):
        return lambda peer: ref.at[lax.rem(peer, 2), lax.div(peer, 2)]

    n63 = pl.ds(0, NG * GW - 1)
    for b in range(3):
        for t, wv in enumerate(waves(b)):
            s2[b, t] = wv.reshape(32, 8, 128)
        if b:
            await_bytes(r2.at[b - 1, n63], away.at[b - 1])
        spread(0, NG * GW, by_row(s2.at[b]), r2.at[b, me], away.at[b], rcv2.at[b])

    points = jnp.broadcast_to(onset_ref[...], (8, 128))
    other = pltpu.roll(points, 64, 1)
    mine = jnp.where(
        yl == 0, jnp.where(low64, points, other), jnp.where(low64, other, points)
    )[0:1]
    mute = lax.broadcasted_iota(jnp.int32, (512, 128), 0) < mine
    mute = jnp.concatenate([mute, mute], axis=1)

    def time_domain(base, count):
        for rq in range(count // 4):
            time_step(base + rq * 4, count)

    def time_step(base, count):
        cols = []
        for u in range(2):
            r = base + u * 2
            a0 = big[pl.ds(r, 64, stride=count), :]
            a1 = big[pl.ds(r + 1, 64, stride=count), :]
            top = jnp.where(low64, a0, pltpu.roll(a1, 64, 1))
            bot = jnp.where(low64, pltpu.roll(a0, 64, 1), a1)
            cols.append(jnp.concatenate([top, bot], axis=0))
        spec = jnp.concatenate(cols, axis=1).astype(BF16)
        trace = jnp.dot(invt_ref[...], spec, preferred_element_type=F32)
        muted = jnp.where(mute, trace, 0.0).astype(BF16)
        again = jnp.dot(fwdt_ref[...], muted, preferred_element_type=F32)
        for u in range(2):
            r = base + u * 2
            top = again[:64, u * 128 : (u + 1) * 128]
            bot = again[64:, u * 128 : (u + 1) * 128]
            tr[pl.ds(r, 64, stride=count), :] = jnp.where(low64, top, pltpu.roll(bot, 64, 1))
            tr[pl.ds(r + 1, 64, stride=count), :] = jnp.where(low64, pltpu.roll(top, 64, 1), bot)

    slot = (lax.rem(me, 2), lax.div(me, 2))
    for b in range(3):
        rows = pl.ds(b * 512, 512)
        await_bytes(r2.at[b], rcv2.at[b])
        big[rows, :] = r2[b].astype(F32).reshape(512, 128)
        time_domain(b * 512, 8)
        s3[b] = tr[rows, :].astype(BF16).reshape(64, 8, 128)
        spread(0, NG * GW, lambda peer: s3.at[b, peer], h3.at[(b, *slot)], back.at[b], rcv3.at[b])

    for b in range(3):
        await_bytes(h3.at[b], rcv3.at[b])
        for t in range(2):
            for u in range(2):
                piece = h3[b, t, pl.ds(u * 16, 16)].astype(F32).reshape(128, 128)
                at = b * TILE + u * 128
                ht[t * 128 : (t + 1) * 128, at : at + 128] = piece.T.astype(BF16)

    @pl.loop(0, NG + 1)
    def _(i):
        @pl.when(i < NG)
        def _():
            g = lax.rem(x + i, NG)
            for b in range(3):
                cols = pl.ds(pl.multiple_of(g * 768 + b * TILE, TILE), TILE)
                pa = jnp.dot(ht[...], mv[0, :, cols], preferred_element_type=F32)
                pb = jnp.dot(ht[...], mv[1, :, cols], preferred_element_type=F32)
                pc = jnp.concatenate(
                    [
                        pa[0:64] + pb[64:128],
                        pa[64:128] - pb[0:64],
                        pa[128:192] + pb[192:256],
                        pa[192:256] - pb[128:192],
                    ],
                    axis=0,
                )
                pv[b * TILE : (b + 1) * TILE, :] = pc.T

            for t in range(2):
                for y in range(2):
                    i0, i1 = [
                        jnp.concatenate(
                            [
                                pv[
                                    (zz * 2 + y) * 48 + u * CH : (zz * 2 + y) * 48 + (u + 1) * CH,
                                    t * 128 : (t + 1) * 128,
                                ]
                                for zz in range(8)
                            ],
                            axis=0,
                        )
                        for u in range(2)
                    ]
                    o0 = jnp.where(low32, i0, pltpu.roll(i1, 32, 1)).astype(BF16)
                    o1 = jnp.where(low32, pltpu.roll(i0, 96, 1), i1).astype(BF16)
                    rs[2 * t, g, y] = o0.reshape(8, CH, 128)
                    rs[2 * t + 1, g, y] = o1.reshape(8, CH, 128)

            for t in range(2):
                send(rs.at[2 * t + (1 - q), g], qv.at[t, g], snd.at[5], rcvq.at[t, g], me, partner)

        @pl.when(i >= 1)
        def _():
            g = lax.rem(x + i - 1, NG)
            for t in range(2):
                await_bytes(qv.at[t, g], rcvq.at[t, g])
                total = rs[2 * t + q, g].astype(F32) + qv[t, g].astype(F32)
                zs[t, g] = total.astype(BF16)
            send(zs.at[1 - yh, g, 1 - yl], zr.at[2, g], snd.at[6], rcvz.at[2, g], beside, ypeer)
            send(zs.at[yh, g, 1 - yl], zr.at[1, g], snd.at[6], rcvz.at[1, g], beside, hf)
            send(zs.at[1 - yh, g, yl], zr.at[0, g], snd.at[6], rcvz.at[0, g], me, ypeer)

    @pl.loop(0, NG)
    def _(i):
        g = lax.rem(x + i, NG)
        for n in range(3):
            await_bytes(zr.at[n, g], rcvz.at[n, g])
        s4[yl, g] = (zs[yh, g, yl].astype(F32) + zr[0, g].astype(F32)).astype(BF16)
        s4[1 - yl, g] = (zr[1, g].astype(F32) + zr[2, g].astype(F32)).astype(BF16)

        @pl.loop(0, 8)
        def _(n):
            tz = lax.rem(z + z_step(n), 8)
            peer = g * GW + tz * 2 + yl
            k = x * GW + z * 2

            @pl.when(i + n > 0)
            def _():
                send(s4.at[0, g, tz], r4.at[k], snd.at[7], rcv4, peer, hf)
                send(s4.at[1, g, tz], r4.at[k + 1], snd.at[7], rcv4, peer, hf)

            @pl.when(i + n == 0)
            def _():
                pltpu.make_async_copy(s4.at[0, g, tz], r4.at[k], rcv4).start()
                pltpu.make_async_copy(s4.at[1, g, tz], r4.at[k + 1], rcv4).start()

    await_bytes(r4, rcv4)

    for b in range(4):
        big[pl.ds(b * 384, 384), :] = r4[pl.ds(b * 16, 16)].astype(F32).reshape(384, 128)

    @pl.loop(0, 12, unroll=4)
    def _(jp):
        j = 2 * jp
        a0 = big[pl.ds(j, 64, stride=CH), :]
        a1 = big[pl.ds(j + 1, 64, stride=CH), :]
        t = jnp.concatenate([a0, a1], axis=0).T
        l0 = jnp.where(low64, t[:64], pltpu.roll(t[64:], 64, 1))
        l1 = jnp.where(low64, pltpu.roll(t[:64], 64, 1), t[64:])
        for s in range(2):
            tr[pl.ds(s * CH + j, 32, stride=48), :] = l0[s * 32 : (s + 1) * 32]
            tr[pl.ds(s * CH + j + 1, 32, stride=48), :] = l1[s * 32 : (s + 1) * 32]

    time = lax.broadcasted_iota(jnp.int32, (48, 512), 1)
    for b in range(4):
        upd = jnp.dot(
            tr[pl.ds(b * 384, 384), :].astype(BF16), inv_ref[...], preferred_element_type=F32
        )
        for n in range(8):
            rows = pl.ds((b * 8 + n) * 48, 48)
            kept = jnp.where(time < onset_smem[hf * 32 + b * 8 + n], upd[n * 48 : (n + 1) * 48], 0.0)
            out_ref[rows, :] = (xv[rows, :].astype(F32) + kept).astype(BF16)

    await_bytes(v1.at[pl.ds(0, 16)], first.at[NG - 1])
    await_bytes(rs.at[pl.ds(0, 3), :, 0], snd.at[1])
    await_bytes(rs.at[pl.ds(0, 2)], snd.at[2])
    await_bytes(r2.at[2, n63], away.at[2])
    for b in range(3):
        await_bytes(s3.at[b, n63], back.at[b])
    await_bytes(rs.at[pl.ds(0, 2)], snd.at[5])
    await_bytes(zr, snd.at[6])
    await_bytes(r4.at[pl.ds(0, 62)], snd.at[7])


def focus_update(focus, kern, tile_mask, onset, points, fwd, fwdt, inv, invt):
    dma = pltpu.SemaphoreType.DMA
    vmem = pl.BlockSpec(memory_space=pltpu.VMEM)
    hbm = pl.BlockSpec(memory_space=pl.ANY)
    smem = pl.BlockSpec(memory_space=pltpu.SMEM)
    chunk = (CH, 128)
    return pl.pallas_call(
        focus_kernel,
        out_shape=pltpu.VMEM((1536, 512), BF16),
        in_specs=[hbm, hbm, smem, hbm, smem, hbm, hbm, hbm, hbm],
        out_specs=vmem,
        scratch_shapes=[
            pltpu.VMEM((1, 128), jnp.int32),
            pltpu.VMEM((512, 128), BF16),
            pltpu.VMEM((128, 512), BF16),
            pltpu.VMEM((128, 512), BF16),
            pltpu.VMEM((512, 128), BF16),
            pltpu.VMEM((1536, 512), BF16),
            pltpu.VMEM((2, 768, 3072), BF16),
            pltpu.VMEM((1536, 128), F32),
            pltpu.VMEM((1536, 128), F32),
            pltpu.VMEM((64, *chunk), BF16),
            pltpu.VMEM((32, *chunk), BF16),
            pltpu.VMEM((4, NG, 2, 8, *chunk), BF16),
            pltpu.VMEM((768, 256), BF16),
            pltpu.VMEM((3, 512, 256), F32),
            pltpu.VMEM((3, 2, 32, 8, 128), BF16),
            pltpu.VMEM((3, 64, 8, 128), BF16),
            pltpu.VMEM((3, 64, 8, 128), BF16),
            pltpu.VMEM((3, 2, 32, 8, 128), BF16),
            pltpu.VMEM((256, 768), BF16),
            pltpu.VMEM((768, 256), F32),
            pltpu.VMEM((4, NG, 2, 8, *chunk), BF16),
            pltpu.VMEM((2, NG, 2, 8, *chunk), BF16),
            pltpu.VMEM((2, NG, 2, 8, *chunk), BF16),
            pltpu.VMEM((3, NG, 8, *chunk), BF16),
            pltpu.VMEM((2, NG, 8, *chunk), BF16),
            pltpu.VMEM((64, *chunk), BF16),
            dma((5,)), dma, dma, dma((8,)), dma((NG,)), dma((3,)), dma((3,)), dma((NG,)), dma((NG,)), dma((3, NG)), dma((4, NG)),
            dma((3,)), dma((3,)), dma((2, NG)), dma((3, NG)), dma,
        ],
        compiler_params=pltpu.CompilerParams(
            collective_id=0, has_side_effects=True, vmem_limit_bytes=50 * 1024 * 1024
        ),
        name="focus_update",
    )(focus, kern, tile_mask, onset, points, fwd, fwdt, inv, invt)


def shards(focus, kernel, onset, tile_mask):
    own_points, local_receivers, length = focus.shape
    fwd, fwdt, inv, invt = make_tables(64, length)
    pinned = functools.partial(pltpu.with_memory_space_constraint, memory_space=pltpu.HBM)
    out = focus_update(
        pinned(focus.reshape(own_points * local_receivers, length)),
        pinned(kernel[0]), pinned(tile_mask), pinned(onset.reshape(1, 128)), onset, *map(pinned, (fwd, fwdt, inv, invt)),
    )
    return out.reshape(focus.shape)


def solution(mesh):
    in_specs = (P("half", "wide", None), P("wide", None, "half", None), P(), P())
    out_specs = P("half", "wide", None)
    return jax.shard_map(shards, mesh=mesh, in_specs=in_specs, out_specs=out_specs, check_vma=False)
```

```python
import functools

import jax
import jax.numpy as jnp
import numpy as np
from jax import lax
from jax.experimental import pallas as pl
from jax.experimental.pallas import tpu as pltpu
from jax.sharding import PartitionSpec as P

TILE = 256
NG = 4
GW = 16
CH = 24
F32 = jnp.float32
BF16 = jnp.bfloat16


def make_tables(bins, length):
    k = np.arange(1, bins + 1)
    t = np.arange(length)
    phase = (t[:, None] * k[None, :] % length).astype(np.float32) * np.float32(
        2.0 * np.pi / length
    )
    table = np.concatenate([np.cos(phase), -np.sin(phase)], axis=1)
    fwd = jnp.asarray(table, F32).astype(BF16)
    invt = jnp.asarray(table * (2.0 / length), F32).astype(BF16)
    return fwd, fwd.T, invt.T, invt


def z_step(n):
    m = lax.div(n, 2)
    return jnp.where(n < 2, 4 * n, jnp.where(lax.rem(n, 2) == 0, m, 8 - m))


def wide_peer(me, d):
    x, loc = lax.div(me, GW), lax.rem(me, GW)
    i, n = lax.div(d, GW), lax.rem(d, GW)
    z, y = lax.div(loc, 2), lax.rem(loc, 2)
    tx = lax.rem(x + i, NG)
    tz = lax.rem(z + z_step(lax.div(n, 2)), 8)
    ty = lax.rem(y + lax.rem(n, 2), 2)
    return tx * GW + tz * 2 + ty


def send(src, dst, ssem, rsem, wide, half):
    pltpu.make_async_remote_copy(
        src_ref=src,
        dst_ref=dst,
        send_sem=ssem,
        recv_sem=rsem,
        device_id={"wide": wide, "half": half},
        device_id_type=pl.DeviceIdType.MESH,
    ).start()


def await_bytes(ref, sem):
    pltpu.make_async_copy(ref, ref, sem).wait()


def focus_kernel(
    focus_hbm, kern_hbm, mask_hbm, onset_hbm, scalar_hbm, fwd_hbm, fwdt_hbm, inv_hbm, invt_hbm,
    out_ref,
    mask_ref, onset_smem, onset_ref, fwd_ref, fwdt_ref, inv_ref, invt_ref, xv, mv, big, tr, v1, b1, r1, fv, acc, s2, r2, s3, h3, ht, pv, rs, qv, zs, zr, s4, r4,
    sem_t, sem_x, sem_m, snd, first, away, back, rcva, rcvb, rel, chip, rcv2, rcv3, rcvq, rcvz, rcv4,
):
    me = lax.axis_index("wide")
    hf = lax.axis_index("half")
    x = lax.div(me, GW)
    yh, q = lax.div(hf, 2), lax.rem(hf, 2)
    partner = yh * 2 + (1 - q)
    ypeer = (1 - yh) * 2 + q
    z, yl = lax.div(lax.rem(me, GW), 2), lax.rem(me, 2)
    beside = x * GW + 2 * z + (1 - yl)
    barrier = pltpu.get_barrier_semaphore()

    @pl.loop(1, NG * GW)
    def _(d):
        pl.semaphore_signal(
            barrier,
            inc=1,
            device_id={"wide": wide_peer(me, d), "half": hf},
            device_id_type=pl.DeviceIdType.MESH,
        )

    for w, other in ((me, partner), (me, ypeer), (beside, ypeer)):
        pl.semaphore_signal(
            barrier,
            inc=1,
            device_id={"wide": w, "half": other},
            device_id_type=pl.DeviceIdType.MESH,
        )

    tables = [
        pltpu.make_async_copy(src, dst, sem_t.at[n])
        for n, (src, dst) in enumerate(
            (
                (fwd_hbm, fwd_ref), (fwdt_hbm, fwdt_ref), (inv_hbm, inv_ref),
                (invt_hbm, invt_ref), (onset_hbm, onset_ref),
                (mask_hbm, mask_ref), (scalar_hbm, onset_smem),
            )
        )
    ]
    tables[0].start()
    copy_x = pltpu.make_async_copy(focus_hbm, xv, sem_x)
    copy_x.start()
    copy_m = pltpu.make_async_copy(kern_hbm, mv, sem_m)
    copy_m.start()
    for table in tables[1:]:
        table.start()

    lane = lax.broadcasted_iota(jnp.int32, (1, 128), 1)
    low64 = lane < 64
    low32 = lax.rem(lane, 64) < 32

    tables[0].wait()
    copy_x.wait()
    for b in range(4):
        rows = pl.ds(b * 384, 384)
        big[rows, :] = jnp.dot(xv[rows, :], fwd_ref[...], preferred_element_type=F32)

    @pl.loop(0, 12, unroll=4)
    def _(jp):
        j = 2 * jp
        a = [
            [big[pl.ds(s * CH + j + jj, 32, stride=48), :] for jj in range(2)]
            for s in range(2)
        ]
        even = [jnp.where(low64, a[s][0], pltpu.roll(a[s][1], 64, 1)) for s in range(2)]
        odd = [jnp.where(low64, pltpu.roll(a[s][0], 64, 1), a[s][1]) for s in range(2)]
        t = jnp.concatenate(even + odd, axis=0).T
        tr[pl.ds(j, 64, stride=CH), :] = t[:64]
        tr[pl.ds(j + 1, 64, stride=CH), :] = t[64:]

    for b in range(4):
        v1[pl.ds(b * 16, 16)] = tr[pl.ds(b * 384, 384), :].astype(BF16).reshape(16, CH, 128)

    pl.semaphore_wait(barrier, NG * GW - 1 + 3)

    here = x * 8 + z
    own_k = here * 2
    pltpu.make_async_copy(v1.at[me], r1.at[hf, x, yl, z], rcva.at[x]).start()
    pltpu.make_async_copy(v1.at[own_k + 1 - yl], b1.at[here], rcvb.at[x]).start()

    for i in range(NG):
        tx = lax.rem(x + i, NG)

        @pl.loop(1 if i == 0 else 0, 8)
        def _(n):
            tz = lax.rem(z + z_step(n), 8)
            k = tx * GW + tz * 2
            peer = k + yl
            send(v1.at[peer], r1.at[hf, x, yl, z], first.at[i], rcva.at[x], peer, hf)
            send(v1.at[k + 1 - yl], b1.at[here], first.at[i], rcvb.at[x], peer, hf)

        if i == 0:
            for table in tables[1:]:
                table.wait()
            copy_m.wait()
        if i < 3:

            @pl.loop(12 * i, 12 * (i + 1))
            def _(n):
                b = n - 12 * i
                keep = mask_ref[hf * 3 + i, b].astype(F32)
                keep = jnp.full((TILE, TILE), keep, F32).astype(BF16)
                rows = pl.ds(i * TILE, TILE)
                cols = pl.ds(pl.multiple_of(b * TILE, TILE), TILE)
                for c in range(2):
                    mv[c, rows, cols] = mv[c, rows, cols] * keep

        if i >= 1:
            await_bytes(v1.at[pl.ds(0, 14 if i == 1 else 16)], first.at[i - 1])

    acc[...] = jnp.zeros_like(acc)
    sign = jnp.where(low64, -1.0, 1.0).astype(F32)

    def slab(g):
        return pl.ds(g * 8, 8)

    def product(g, b):
        rows = pl.ds(pl.multiple_of(b * TILE, TILE), TILE)
        cols = pl.ds(pl.multiple_of(g * 768, 768), 768)
        lhs = jnp.concatenate([mv[0, rows, cols], mv[1, rows, cols]], axis=0)
        return jnp.dot(lhs, fv[...], preferred_element_type=F32)

    @pl.loop(0, NG)
    def _(i):
        g = lax.rem(x - i + NG, NG)
        own = r1.at[hf, g, yl]
        await_bytes(own, rcva.at[g])
        send(own, own, snd.at[1], rel.at[0, g], me, ypeer)
        await_bytes(b1.at[slab(g)], rcvb.at[g])
        send(b1.at[slab(g)], own, snd.at[1], rel.at[1, g], beside, hf)
        send(b1.at[slab(g)], own, snd.at[1], rel.at[2, g], beside, ypeer)
        send(own, own, snd.at[2], chip.at[0, g], me, partner)

    @pl.loop(0, NG + 1)
    def _(i):
        @pl.when(i < NG)
        def _():
            g = lax.rem(x - i + NG, NG)
            for n, (h, y) in enumerate(((ypeer, yl), (hf, 1 - yl), (ypeer, 1 - yl))):
                got = r1.at[h, g, y]
                await_bytes(got, rel.at[n, g])
                send(got, got, snd.at[2], chip.at[n + 1, g], me, partner)

        @pl.when(i >= 1)
        def _():
            g = lax.rem(x - i + 1 + NG, NG)
            diag = (1 - yh) * 2 + (1 - q)
            for n, (h, y) in enumerate(
                ((partner, yl), (diag, yl), (partner, 1 - yl), (diag, 1 - yl))
            ):
                await_bytes(r1.at[h, g, y], chip.at[n, g])

            for t in range(2):
                for y in range(2):
                    b0 = r1[2 * t, g, y].astype(F32).reshape(192, 128)
                    b1_ = r1[2 * t + 1, g, y].astype(F32).reshape(192, 128)
                    o0 = jnp.where(low32, b0, pltpu.roll(b1_, 32, 1))
                    o1 = jnp.where(low32, pltpu.roll(b0, 96, 1), b1_)
                    for zz in range(8):
                        at = slice(zz * CH, (zz + 1) * CH)
                        rows = (zz * 2 + y) * 48
                        fv[rows : rows + 48, t * 128 : (t + 1) * 128] = jnp.concatenate(
                            [o0[at], o1[at]], axis=0
                        ).astype(BF16)

            @pl.when(i < NG)
            def _():
                @pl.loop(0, 3)
                def _(b):
                    acc[b] += product(g, b)

    def waves(b):
        full = acc[b] + product(lax.rem(x + 1, NG), b)
        return [
            (
                full[:TILE, t * 128 : (t + 1) * 128]
                + sign * pltpu.roll(full[TILE:, t * 128 : (t + 1) * 128], 64, 1)
            ).astype(BF16)
            for t in range(2)
        ]

    def spread(first, last, src_of, dst, ssem, rsem):
        @pl.loop(first, last)
        def _(d):
            peer = wide_peer(me, d)

            @pl.when(d > 0)
            def _():
                send(src_of(peer), dst, ssem, rsem, peer, hf)

            @pl.when(d == 0)
            def _():
                pltpu.make_async_copy(src_of(peer), dst, rsem).start()

    def by_row(ref):
        return lambda peer: ref.at[lax.rem(peer, 2), lax.div(peer, 2)]

    n63 = pl.ds(0, NG * GW - 1)
    for b in range(3):
        for t, wv in enumerate(waves(b)):
            s2[b, t] = wv.reshape(32, 8, 128)
        if b:
            await_bytes(r2.at[b - 1, n63], away.at[b - 1])
        spread(0, NG * GW, by_row(s2.at[b]), r2.at[b, me], away.at[b], rcv2.at[b])

    points = jnp.broadcast_to(onset_ref[...], (8, 128))
    other = pltpu.roll(points, 64, 1)
    mine = jnp.where(
        yl == 0, jnp.where(low64, points, other), jnp.where(low64, other, points)
    )[0:1]
    mute = lax.broadcasted_iota(jnp.int32, (512, 128), 0) < mine
    mute = jnp.concatenate([mute, mute], axis=1)

    def time_domain(base, count):
        for rq in range(count // 4):
            time_step(base + rq * 4, count)

    def time_step(base, count):
        cols = []
        for u in range(2):
            r = base + u * 2
            a0 = big[pl.ds(r, 64, stride=count), :]
            a1 = big[pl.ds(r + 1, 64, stride=count), :]
            top = jnp.where(low64, a0, pltpu.roll(a1, 64, 1))
            bot = jnp.where(low64, pltpu.roll(a0, 64, 1), a1)
            cols.append(jnp.concatenate([top, bot], axis=0))
        spec = jnp.concatenate(cols, axis=1).astype(BF16)
        trace = jnp.dot(invt_ref[...], spec, preferred_element_type=F32)
        muted = jnp.where(mute, trace, 0.0).astype(BF16)
        again = jnp.dot(fwdt_ref[...], muted, preferred_element_type=F32)
        for u in range(2):
            r = base + u * 2
            top = again[:64, u * 128 : (u + 1) * 128]
            bot = again[64:, u * 128 : (u + 1) * 128]
            tr[pl.ds(r, 64, stride=count), :] = jnp.where(low64, top, pltpu.roll(bot, 64, 1))
            tr[pl.ds(r + 1, 64, stride=count), :] = jnp.where(low64, pltpu.roll(top, 64, 1), bot)

    slot = (lax.rem(me, 2), lax.div(me, 2))
    for b in range(3):
        rows = pl.ds(b * 512, 512)
        await_bytes(r2.at[b], rcv2.at[b])
        big[rows, :] = r2[b].astype(F32).reshape(512, 128)
        time_domain(b * 512, 8)
        s3[b] = tr[rows, :].astype(BF16).reshape(64, 8, 128)
        spread(0, NG * GW, lambda peer: s3.at[b, peer], h3.at[(b, *slot)], back.at[b], rcv3.at[b])

    for b in range(3):
        await_bytes(h3.at[b], rcv3.at[b])
        for t in range(2):
            for u in range(2):
                piece = h3[b, t, pl.ds(u * 16, 16)].astype(F32).reshape(128, 128)
                at = b * TILE + u * 128
                ht[t * 128 : (t + 1) * 128, at : at + 128] = piece.T.astype(BF16)

    @pl.loop(0, NG + 1)
    def _(i):
        @pl.when(i < NG)
        def _():
            g = lax.rem(x + i, NG)
            for b in range(3):
                cols = pl.ds(pl.multiple_of(g * 768 + b * TILE, TILE), TILE)
                pa = jnp.dot(ht[...], mv[0, :, cols], preferred_element_type=F32)
                pb = jnp.dot(ht[...], mv[1, :, cols], preferred_element_type=F32)
                pc = jnp.concatenate(
                    [
                        pa[0:64] + pb[64:128],
                        pa[64:128] - pb[0:64],
                        pa[128:192] + pb[192:256],
                        pa[192:256] - pb[128:192],
                    ],
                    axis=0,
                )
                pv[b * TILE : (b + 1) * TILE, :] = pc.T

            for t in range(2):
                for y in range(2):
                    i0, i1 = [
                        jnp.concatenate(
                            [
                                pv[
                                    (zz * 2 + y) * 48 + u * CH : (zz * 2 + y) * 48 + (u + 1) * CH,
                                    t * 128 : (t + 1) * 128,
                                ]
                                for zz in range(8)
                            ],
                            axis=0,
                        )
                        for u in range(2)
                    ]
                    o0 = jnp.where(low32, i0, pltpu.roll(i1, 32, 1)).astype(BF16)
                    o1 = jnp.where(low32, pltpu.roll(i0, 96, 1), i1).astype(BF16)
                    rs[2 * t, g, y] = o0.reshape(8, CH, 128)
                    rs[2 * t + 1, g, y] = o1.reshape(8, CH, 128)

            for t in range(2):
                send(rs.at[2 * t + (1 - q), g], qv.at[t, g], snd.at[5], rcvq.at[t, g], me, partner)

        @pl.when(i >= 1)
        def _():
            g = lax.rem(x + i - 1, NG)
            for t in range(2):
                await_bytes(qv.at[t, g], rcvq.at[t, g])
                total = rs[2 * t + q, g].astype(F32) + qv[t, g].astype(F32)
                zs[t, g] = total.astype(BF16)
            send(zs.at[1 - yh, g, 1 - yl], zr.at[2, g], snd.at[6], rcvz.at[2, g], beside, ypeer)
            send(zs.at[yh, g, 1 - yl], zr.at[1, g], snd.at[6], rcvz.at[1, g], beside, hf)
            send(zs.at[1 - yh, g, yl], zr.at[0, g], snd.at[6], rcvz.at[0, g], me, ypeer)

    @pl.loop(0, NG)
    def _(i):
        g = lax.rem(x + i, NG)
        for n in range(3):
            await_bytes(zr.at[n, g], rcvz.at[n, g])
        s4[yl, g] = (zs[yh, g, yl].astype(F32) + zr[0, g].astype(F32)).astype(BF16)
        s4[1 - yl, g] = (zr[1, g].astype(F32) + zr[2, g].astype(F32)).astype(BF16)

        @pl.loop(0, 8)
        def _(n):
            tz = lax.rem(z + z_step(n), 8)
            peer = g * GW + tz * 2 + yl
            k = x * GW + z * 2

            @pl.when(i + n > 0)
            def _():
                send(s4.at[0, g, tz], r4.at[k], snd.at[7], rcv4, peer, hf)
                send(s4.at[1, g, tz], r4.at[k + 1], snd.at[7], rcv4, peer, hf)

            @pl.when(i + n == 0)
            def _():
                pltpu.make_async_copy(s4.at[0, g, tz], r4.at[k], rcv4).start()
                pltpu.make_async_copy(s4.at[1, g, tz], r4.at[k + 1], rcv4).start()

    await_bytes(r4, rcv4)

    for b in range(4):
        big[pl.ds(b * 384, 384), :] = r4[pl.ds(b * 16, 16)].astype(F32).reshape(384, 128)

    @pl.loop(0, 12, unroll=4)
    def _(jp):
        j = 2 * jp
        a0 = big[pl.ds(j, 64, stride=CH), :]
        a1 = big[pl.ds(j + 1, 64, stride=CH), :]
        t = jnp.concatenate([a0, a1], axis=0).T
        l0 = jnp.where(low64, t[:64], pltpu.roll(t[64:], 64, 1))
        l1 = jnp.where(low64, pltpu.roll(t[:64], 64, 1), t[64:])
        for s in range(2):
            tr[pl.ds(s * CH + j, 32, stride=48), :] = l0[s * 32 : (s + 1) * 32]
            tr[pl.ds(s * CH + j + 1, 32, stride=48), :] = l1[s * 32 : (s + 1) * 32]

    time = lax.broadcasted_iota(jnp.int32, (48, 512), 1)
    for b in range(4):
        upd = jnp.dot(
            tr[pl.ds(b * 384, 384), :].astype(BF16), inv_ref[...], preferred_element_type=F32
        )
        for n in range(8):
            rows = pl.ds((b * 8 + n) * 48, 48)
            kept = jnp.where(time < onset_smem[hf * 32 + b * 8 + n], upd[n * 48 : (n + 1) * 48], 0.0)
            out_ref[rows, :] = (xv[rows, :].astype(F32) + kept).astype(BF16)

    await_bytes(v1.at[pl.ds(0, 16)], first.at[NG - 1])
    await_bytes(rs.at[pl.ds(0, 3), :, 0], snd.at[1])
    await_bytes(rs.at[pl.ds(0, 2)], snd.at[2])
    await_bytes(r2.at[2, n63], away.at[2])
    for b in range(3):
        await_bytes(s3.at[b, n63], back.at[b])
    await_bytes(rs.at[pl.ds(0, 2)], snd.at[5])
    await_bytes(zr, snd.at[6])
    await_bytes(r4.at[pl.ds(0, 62)], snd.at[7])


def focus_update(focus, kern, tile_mask, onset, points, fwd, fwdt, inv, invt):
    dma = pltpu.SemaphoreType.DMA
    vmem = pl.BlockSpec(memory_space=pltpu.VMEM)
    hbm = pl.BlockSpec(memory_space=pl.ANY)
    chunk = (CH, 128)
    return pl.pallas_call(
        focus_kernel,
        out_shape=pltpu.VMEM((1536, 512), BF16),
        in_specs=[hbm, hbm, hbm, hbm, hbm, hbm, hbm, hbm, hbm],
        out_specs=vmem,
        scratch_shapes=[
            pltpu.SMEM((12, 12), jnp.int32),
            pltpu.SMEM((128,), jnp.int32),
            pltpu.VMEM((1, 128), jnp.int32),
            pltpu.VMEM((512, 128), BF16),
            pltpu.VMEM((128, 512), BF16),
            pltpu.VMEM((128, 512), BF16),
            pltpu.VMEM((512, 128), BF16),
            pltpu.VMEM((1536, 512), BF16),
            pltpu.VMEM((2, 768, 3072), BF16),
            pltpu.VMEM((1536, 128), F32),
            pltpu.VMEM((1536, 128), F32),
            pltpu.VMEM((64, *chunk), BF16),
            pltpu.VMEM((32, *chunk), BF16),
            pltpu.VMEM((4, NG, 2, 8, *chunk), BF16),
            pltpu.VMEM((768, 256), BF16),
            pltpu.VMEM((3, 512, 256), F32),
            pltpu.VMEM((3, 2, 32, 8, 128), BF16),
            pltpu.VMEM((3, 64, 8, 128), BF16),
            pltpu.VMEM((3, 64, 8, 128), BF16),
            pltpu.VMEM((3, 2, 32, 8, 128), BF16),
            pltpu.VMEM((256, 768), BF16),
            pltpu.VMEM((768, 256), F32),
            pltpu.VMEM((4, NG, 2, 8, *chunk), BF16),
            pltpu.VMEM((2, NG, 2, 8, *chunk), BF16),
            pltpu.VMEM((2, NG, 2, 8, *chunk), BF16),
            pltpu.VMEM((3, NG, 8, *chunk), BF16),
            pltpu.VMEM((2, NG, 8, *chunk), BF16),
            pltpu.VMEM((64, *chunk), BF16),
            dma((7,)), dma, dma, dma((8,)), dma((NG,)), dma((3,)), dma((3,)), dma((NG,)), dma((NG,)), dma((3, NG)), dma((4, NG)),
            dma((3,)), dma((3,)), dma((2, NG)), dma((3, NG)), dma,
        ],
        compiler_params=pltpu.CompilerParams(
            collective_id=0, has_side_effects=True, vmem_limit_bytes=50 * 1024 * 1024
        ),
        name="focus_update",
    )(focus, kern, tile_mask, onset, points, fwd, fwdt, inv, invt)


def shards(focus, kernel, onset, tile_mask):
    own_points, local_receivers, length = focus.shape
    fwd, fwdt, inv, invt = make_tables(64, length)
    pinned = functools.partial(pltpu.with_memory_space_constraint, memory_space=pltpu.HBM)
    out = focus_update(
        pinned(focus.reshape(own_points * local_receivers, length)),
        pinned(kernel[0]), pinned(tile_mask), pinned(onset.reshape(1, 128)), pinned(onset), *map(pinned, (fwd, fwdt, inv, invt)),
    )
    return out.reshape(focus.shape)


def solution(mesh):
    in_specs = (P("half", "wide", None), P("wide", None, "half", None), P(), P())
    out_specs = P("half", "wide", None)
    return jax.shard_map(shards, mesh=mesh, in_specs=in_specs, out_specs=out_specs, check_vma=False)
```
